128 devices in a mesh: sec: 2 (over x_lo), batch: 32 (over z, y, core), head: 2 (over x_hi).
Axes of the slice: x: 4 (x_hi: 2, x_lo: 2; x = x_hi * 2 + x_lo), y: 4, z: 4, core: 2. Of those that a mesh axis runs over, the one named last changes fastest.
Arguments:
- hidden_in: bfloat16 [1024, 7168], P('batch'), may hold values from -6 to 6
- queries: bfloat16 [1024, 128, 576], P('batch', ('sec', 'head')), may hold values from -8 to 8
- latent_cache: bfloat16 [1024, 192, 576], P('batch'), may hold values from -8 to 8
- new_latent: bfloat16 [1024, 576], P('batch'), may hold values from -8 to 8
- cache_lengths: int32 [1024], P('batch'), may hold values from 1 to 192, 98304 in all
- value_up: bfloat16 [128, 512, 128], P(('sec', 'head')), may hold values from -0.25 to 0.25
- out_proj: bfloat16 [16384, 7168], P(('sec', 'head'), 'batch'), may hold values from -0.046875 to 0.046875
- norm_gain: float32 [7168], replicated, may hold values from 0.1 to 1.9
- router: bfloat16 [7168, 32], replicated, may hold values from -0.03125 to 0.03125
- expert_ids: int32 [1024, 8], P('batch'), may hold values from 0 to 31, all different within a row; in each aligned block of 32 rows (0 to 31, 32 to 63, ...) at most 16 rows name the same one
- w_gate_up: bfloat16 [32, 7168, 2, 1024], P('batch', None, None, ('sec', 'head')), may hold values from -0.0625 to 0.0625
- w_down: bfloat16 [32, 1024, 7168], P('batch', ('sec', 'head')), may hold values from -0.1875 to 0.1875
Outputs:
- mixed_out: bfloat16 [1024, 7168], P('batch', ('sec', 'head'))
The draws below stay inside these ranges and needn't reach their ends.
Inputs may be any that keep to these rules, and one draw needn't show every extreme that they name: `expert_ids`: each row names 8 different experts. Among the 32 rows of one index of batch (aligned blocks) no expert is named by more than 16 rows, a bound that some block reaches. `cache_lengths`: the lengths of all rows add up to 98304, and one row has exactly 192.
All inputs are finite; a program needn't handle non-finite values. No bound on the sum of `cache_lengths` on one device may be relied on, other than what follows from the above.
Results may differ from the reference program's by a relative error of at most 0.007.
Values may be sent and summed in bfloat16 or wider, within the bound.
A program may use at most 128 MiB of HBM per device.

```python
import math
import jax
import jax.numpy as jnp
import numpy as np
from jax import lax

D = 7168
HEADS = 128
LAT = 512
HD = 128
QKD = 192
FF = 1024
TOP = 8
TOK_DEV = 32
CTX = 192
TOKENS = 1024
EXPERTS = 32
KVW = 576
CAP = 16
N_BATCH = 32


def draw_latent_cache(key, part):
    noise = jnp.clip(jax.random.normal(jax.random.fold_in(key, 1), (TOKENS, CTX, KVW), jnp.float32), -4.0, 4.0)
    return noise.astype(jnp.bfloat16)


def draw_new_latent(key, part):
    noise = jnp.clip(jax.random.normal(jax.random.fold_in(key, 2), (TOKENS, KVW), jnp.float32), -4.0, 4.0)
    return noise.astype(jnp.bfloat16)


def draw_queries(key, part):
    noise = jnp.clip(jax.random.normal(jax.random.fold_in(key, 3), (TOKENS, HEADS, KVW), jnp.float32), -4.0, 4.0)
    return noise.astype(jnp.bfloat16)


def levels(own_key, extent, cuts, smallest, top_value):
    def one(axis_at, parts):
        heights = jax.random.uniform(jax.random.fold_in(jax.random.fold_in(own_key, 6), axis_at), (parts,), jnp.float32, smallest / len(cuts), top_value / len(cuts))
        return jnp.repeat(jnp.exp(heights), extent[axis_at] // parts).reshape((-1,) + (1,) * (len(extent) - axis_at - 1))

    loudness = one(*cuts[0])
    for cut in cuts[1:]:
        loudness = loudness * one(*cut)
    return loudness


def length_profile(number_of, total, most, skew):
    weights = [(1 << 20) // math.isqrt(rank ** skew) + 1 for rank in range(2, number_of + 1)]
    spare, given = total - most - (number_of - 1), [1] * (number_of - 1)
    while spare > 0:
        free = [i for i in range(number_of - 1) if given[i] < most]
        pool, remaining = sum([weights[i] for i in free]), spare
        for i in free:
            addition = min(most - given[i], max(1, remaining * weights[i] // pool), spare)
            given[i] = given[i] + addition
            spare = spare - addition
    return np.array([most] + given)


def uneven(key, count, total, most, skew):
    if count == 2:
        one = jax.random.randint(key, (), max(1, total - most), min(most, total - 1) + 1)
        return jnp.stack([one, total - one])
    lengths = jnp.asarray(length_profile(count, total, most, skew), jnp.int32)
    twos = (count - 1) // 2
    source_of, sink = lengths[1:1 + 2 * twos:2], lengths[2:2 + 2 * twos:2]
    room = jnp.minimum(source_of - 1, most - sink)
    moved = jax.random.randint(jax.random.fold_in(key, 1), (twos,), 0, 1 << 20) % (room + 1)
    lengths = lengths.at[1:1 + 2 * twos:2].set(source_of - moved).at[2:2 + 2 * twos:2].set(sink + moved)
    return lengths[jax.random.permutation(jax.random.fold_in(key, 2), count)]


def shared_out(stream_key, own, number, rows, count, top, limit, lean):
    order = jax.random.permutation(stream_key, count)
    packed, usual = load_shares(count, rows * top, limit, lean, True), load_shares(count, rows * top, limit, lean, False)
    places = jnp.arange(count)

    def named(sizes, offset_by):
        used = int((sizes > 0).sum())
        fixed = max(1, used // 4)
        moved = fixed + (places - fixed + offset_by * (used - fixed)) % max(1, count - fixed)
        return jnp.zeros((count,), jnp.int32).at[order[jnp.where(places < fixed, places, moved)]].set(jnp.asarray(sizes, jnp.int32))

    sizes = jnp.where(number % 4 == 0, named(packed, number // 4), named(usual, number - number // 4 - 1))
    mixed = jax.random.permutation(jax.random.fold_in(own, 3), count)
    donor, receiver = mixed[0:count // 2 * 2:2], mixed[1:count // 2 * 2:2]
    margin = jnp.minimum(sizes[donor] - 1, limit - sizes[receiver]) // 2
    margin = jnp.where((donor == order[0]) | (receiver == order[0]) | (sizes[receiver] == 0), 0, jnp.maximum(margin, 0))
    moved = jax.random.randint(jax.random.fold_in(own, 4), (count // 2,), 0, 1 << 20) % (margin + 1)
    sizes = sizes.at[donor].add(-moved).at[receiver].add(moved)
    members = jnp.searchsorted(jnp.cumsum(sizes), jnp.arange(rows * top), side="right").astype(jnp.int32)
    table = members.reshape(top, rows).T
    table = table[jax.random.permutation(jax.random.fold_in(own, 1), rows)]
    offset_by = jax.random.randint(jax.random.fold_in(own, 2), (rows, 1), 0, top)
    return jnp.take_along_axis(table, (jnp.arange(top)[None, :] + offset_by) % top, axis=1)


def load_shares(amount, total, limit, lean, full):
    portions = [(1 << 20) // math.isqrt(rank ** lean) + 1 for rank in range(1, amount + 1)]
    largest = limit if full else min(limit, max(-(-total // amount), total * portions[0] // sum(portions)))
    least = 1 if total - largest >= amount - 1 else 0
    holding, spare = [largest] + [least] * (amount - 1), total - largest - least * (amount - 1)
    while spare > 0:
        free = [i for i in range(1, amount) if holding[i] < largest] or [i for i in range(1, amount) if holding[i] < limit]
        pool, budget = sum([portions[i] for i in free]), spare
        for i in free:
            more = min(limit - holding[i], max(1, budget * portions[i] // pool), spare)
            holding[i] = holding[i] + more
            spare = spare - more
    return np.array(holding)


def centred(key, shape, scale, bound, cuts=(), kind=jnp.bfloat16):
    entries = scale * jax.random.normal(key, shape, jnp.float32)
    if cuts:
        entries = entries * levels(key, shape, cuts, -0.22, 0.18)
    return jnp.clip(entries, -bound, bound).astype(kind)


def setup_inputs(seed: int = 0) -> dict:
    splits = jax.random.split(jax.random.key(seed), 13)
    hidden_in = centred(splits[0], (TOKENS, D), 1.0, 6.0, ((0, 32),))
    queries = draw_queries(jax.random.fold_in(splits[12], 71), 0)
    latent_cache = draw_latent_cache(jax.random.fold_in(splits[12], 71), 0)
    new_latent = draw_new_latent(jax.random.fold_in(splits[12], 71), 0)
    cache_lengths = uneven(splits[4], TOKENS, TOKENS * CTX // 2, CTX, 2).astype(jnp.int32)
    value_up = centred(splits[5], (HEADS, LAT, HD), LAT ** -0.5, 0.25, ((0, 4),))
    out_proj = centred(splits[6], (HEADS * HD, D), (HEADS * HD) ** -0.5, 0.046875, ((0, 4), (1, 32)))
    norm_gain = jnp.clip(1.0 + 0.18 * jax.random.normal(splits[7], (D,), jnp.float32), 0.1, 1.9)
    router = centred(splits[8], (D, EXPERTS), (4 * D) ** -0.5, 0.03125)
    expert_ids_keys = jax.random.split(jax.random.fold_in(splits[9], 1), TOKENS // TOK_DEV)
    expert_ids_turns = jax.random.permutation(jax.random.fold_in(splits[9], 3), TOKENS // TOK_DEV)
    expert_ids = jax.vmap(lambda own, number: shared_out(jax.random.fold_in(splits[9], 2), own, number, TOK_DEV, EXPERTS, TOP, CAP, 2))(expert_ids_keys, expert_ids_turns).reshape((TOKENS, TOP))
    w_gate_up = centred(splits[10], (EXPERTS, D, 2, FF), D ** -0.5, 0.0625, ((0, 32), (3, 4)))
    w_down = centred(splits[11], (EXPERTS, FF, D), FF ** -0.5, 0.1875, ((0, 32), (1, 4)))
    return {"hidden_in": hidden_in, "queries": queries, "latent_cache": latent_cache, "new_latent": new_latent, "cache_lengths": cache_lengths, "value_up": value_up, "out_proj": out_proj, "norm_gain": norm_gain, "router": router, "expert_ids": expert_ids, "w_gate_up": w_gate_up, "w_down": w_down}


norm_epsilon = 1e-06
route_scale = 2.5

def reference(hidden_in, queries, latent_cache, new_latent, cache_lengths, value_up, out_proj, norm_gain, router, expert_ids, w_gate_up, w_down):
    score_scale = QKD ** (-0.5)
    query_full = queries.astype(jnp.float32)
    cache_full = latent_cache.astype(jnp.float32)
    newest = new_latent.astype(jnp.float32)
    scores = jnp.einsum('thk,tjk->thj', query_full, cache_full) * score_scale
    own_score = jnp.einsum('thk,tk->th', query_full, newest) * score_scale
    positions = jnp.arange(CTX, dtype=jnp.int32)
    in_cache = positions[None, None, :] < cache_lengths[:, None, None]
    scores = jnp.where(in_cache, scores, -jnp.inf)
    top_score = jnp.maximum(lax.optimization_barrier(jnp.max(scores, axis=2)), own_score)
    cache_exp = jnp.exp(scores - top_score[:, :, None])
    own_exp = jnp.exp(own_score - top_score)
    softmax_sum = lax.optimization_barrier(jnp.sum(cache_exp, axis=2)) + own_exp
    cache_weights = (cache_exp / softmax_sum[:, :, None]).astype(jnp.bfloat16)
    own_weights = (own_exp / softmax_sum).astype(jnp.bfloat16)
    latent_out = jnp.einsum('thj,tjc->thc', cache_weights.astype(jnp.float32), cache_full[:, :, :LAT])
    latent_out = latent_out + own_weights.astype(jnp.float32)[:, :, None] * newest[:, None, :LAT]
    latent_out = latent_out.astype(jnp.bfloat16)
    head_out = jnp.einsum('thc,hcd->thd', latent_out.astype(jnp.float32), value_up.astype(jnp.float32))
    head_out = head_out.astype(jnp.bfloat16).reshape(TOKENS, HEADS * HD)
    attention = jnp.dot(head_out, out_proj, preferred_element_type=jnp.float32)
    residual = hidden_in.astype(jnp.float32) + attention
    mean_square = lax.optimization_barrier(jnp.mean(residual * residual, axis=1, keepdims=True))
    normed = (residual * lax.rsqrt(mean_square + norm_epsilon) * norm_gain).astype(jnp.bfloat16)
    logits = jnp.dot(normed, router, preferred_element_type=jnp.float32)
    affinity = jax.nn.sigmoid(logits)
    picked = jnp.take_along_axis(affinity, expert_ids, axis=1)
    route_weights = route_scale * picked / lax.optimization_barrier(jnp.sum(picked, axis=1, keepdims=True))
    slot_limit = N_BATCH * CAP

    def one_expert(mixture, expert):
        hit_mask = expert_ids == expert
        token_weight = lax.optimization_barrier(jnp.sum(jnp.where(hit_mask, route_weights, jnp.zeros_like(route_weights)), axis=1))
        routed = jnp.any(hit_mask, axis=1)
        chosen = jnp.nonzero(routed, size=slot_limit, fill_value=0)[0].astype(jnp.int32)
        occupied = jnp.arange(slot_limit, dtype=jnp.int32) < jnp.sum(routed.astype(jnp.int32))
        inputs = normed[chosen]
        gate_up = jnp.dot(inputs, w_gate_up[expert].reshape(D, 2 * FF), preferred_element_type=jnp.float32)
        activated = (jax.nn.silu(gate_up[:, :FF]) * gate_up[:, FF:]).astype(jnp.bfloat16)
        expert_out = jnp.dot(activated, w_down[expert], preferred_element_type=jnp.float32)
        slot_weight = jnp.where(occupied, token_weight[chosen], jnp.zeros_like(token_weight[chosen]))
        mixture = mixture.at[chosen].add(slot_weight[:, None] * expert_out)
        return (mixture, None)
    mixture, unused = lax.scan(one_expert, jnp.zeros((TOKENS, D), jnp.float32), jnp.arange(EXPERTS, dtype=jnp.int32))
    return (residual + mixture).astype(jnp.bfloat16)
```

```python
import jax
import jax.numpy as jnp
from jax import lax
from jax.experimental import pallas as pl
from jax.experimental.pallas import tpu as pltpu
from jax.sharding import PartitionSpec as P

QKD = 192
TOP = 8
norm_epsilon = 1e-06
route_scale = 2.5

BF16, F32 = jnp.bfloat16, jnp.float32
MESH = pl.DeviceIdType.MESH
PARTS = ((0, 640, 1280), (1280, 1920, 2560), (2560, 3200, 3712))
HALF = 3584


def dot(a, b):
    return lax.dot_general(a, b, (((1,), (0,)), ((), ())), preferred_element_type=F32)


def dot_t(a, b):
    return lax.dot_general(a, b, (((1,), (1,)), ((), ())), preferred_element_type=F32)


def layer_kernel(
    head_hbm, wo_hbm, wgu_hbm, wd_hbm, hid_ref, gain_ref, router_ref, ids_ref,
    out_ref,
    H, WO, ACC, PS, RX, SS, RY, MS, MR, RF, RL, X, WGU, GU, WD, A, Y0, Y1, OWN, R0, R1, T0, T1, Q0, Q1,
    ring_s, ring_r, bx_s, bx_r, by_s, by_r, m_s, m_r, rl_s, rl_r, wo_s, wo_r, wg_s, wg_r, wd_s, wd_r, wf_s, wf_r,
    y1_s, y1_r, y2_s, y2_r, loc,
):
    sec = lax.axis_index("sec")
    head = lax.axis_index("head")
    batch = lax.axis_index("batch")
    core = batch % 2
    y = (batch // 2) % 4
    z = batch // 8
    x = head * 2 + sec
    p = z * 4 + y

    def at(zz=None, yy=None, cc=None, xx=None):
        zz = z if zz is None else zz
        yy = y if yy is None else yy
        cc = core if cc is None else cc
        xx = x if xx is None else xx
        return (xx % 2, zz * 8 + yy * 2 + cc, xx // 2)

    def rcopy(src, dst, send, recv, to):
        return pltpu.make_async_remote_copy(
            src_ref=src, dst_ref=dst, send_sem=send, recv_sem=recv, device_id=to, device_id_type=MESH
        )

    def lcopy(src, dst, k):
        return pltpu.make_async_copy(src, dst, loc.at[k])

    sends = []

    def go(copy):
        copy.start()
        sends.append(copy)
        return copy

    own_head = lcopy(head_hbm, H.at[z, y], 0)
    own_head.start()
    own_wo = lcopy(wo_hbm, WO.at[core], 1)
    own_wo.start()

    def own_wgu_step(i, carry):
        for h in range(2):
            lcopy(wgu_hbm.at[i, h], WGU.at[core, h, pl.ds(pl.multiple_of(i * 224, 16), 224)], 2).start()
        return carry

    lax.fori_loop(0, 16, own_wgu_step, 0)

    def wd_cols(xx):
        s = (xx % 2) * 2 + xx // 2
        return wd_hbm.at[:, pl.ds(pl.multiple_of(s * 1792, 128), 1792)]

    own_wd = lcopy(wd_cols(x), WD.at[x, core], 3)
    own_wd.start()

    barrier = pltpu.get_barrier_semaphore()

    def greet(to):
        pl.semaphore_signal(barrier, inc=1, device_id=to, device_id_type=MESH)

    greet(at(cc=1 - core))
    for d in range(1, 4):
        greet(at(xx=(x + d) % 4))
    for d in range(1, 16):
        q = (p + d) % 16
        greet(at(zz=q // 4, yy=q % 4))
    pl.semaphore_wait(barrier, 19)

    dims = {"z": z, "y": y, "x": x}

    def neighbour(dim, d):
        i = (dims[dim] + d) % 4
        return at(zz=i) if dim == "z" else at(yy=i) if dim == "y" else at(xx=i)

    class Ring:
        def __init__(self, k, dim, full, low, high):
            self.k, self.dim, self.full, self.low, self.high = k, dim, full, low, high

        def copy(self, part, i, d, j):
            i = (dims[self.dim] + i) % 4
            return rcopy(part(i), part(i), ring_s.at[self.k, j], ring_r.at[self.k, j], neighbour(self.dim, d))

        def start(self):
            self.up = go(self.copy(self.full, 0, 1, 0))
            self.down = go(self.copy(self.full, 0, 3, 1))

        def forward(self):
            self.up.wait_recv()
            self.far_up = go(self.copy(self.low, 3, 1, 2))
            self.down.wait_recv()
            self.far_down = go(self.copy(self.high, 1, 3, 3))

        def finish(self):
            self.far_up.wait_recv()
            self.far_down.wait_recv()

    def head_ring(k, dim, half, other_full):
        def view(rows):
            def part(i):
                cols = pl.ds(half * 2048, 2048)
                if dim == "z":
                    return H.at[i, :, rows, cols] if other_full else H.at[i, y, rows, cols]
                return H.at[:, i, rows, cols] if other_full else H.at[z, i, rows, cols]

            return part

        return Ring(k, dim, view(pl.ds(0, 32)), view(pl.ds(0, 16)), view(pl.ds(16, 16)))

    h0a, h0b = head_ring(0, "y", 0, False), head_ring(1, "z", 0, True)
    h1a, h1b = head_ring(2, "z", 1, False), head_ring(3, "y", 1, True)

    own_head.wait()
    h0a.start()
    h1a.start()
    other_core = at(cc=1 - core)
    send_wo = go(rcopy(wo_hbm, WO.at[core], wo_s.at[0], wo_r.at[0], other_core))
    send_wd = []
    for d in (1, 3, 2):
        xx = (x + d) % 4
        send_wd.append(go(rcopy(wd_cols(xx), WD.at[x, core], wd_s.at[d - 1], wd_r.at[d - 1], at(xx=xx))))

    def far_wgu(i, h):
        return rcopy(
            wgu_hbm.at[i, h], WGU.at[core, h, pl.ds(pl.multiple_of(i * 224, 16), 224)], wg_s.at[0], wg_r.at[0], other_core
        )

    def far_wgu_step(i, carry):
        for h in range(2):
            far_wgu(i, h).start()
        return carry

    lax.fori_loop(0, 16, far_wgu_step, 0)
    wgu_all = rcopy(WGU.at[core], WGU.at[core], wg_s.at[0], wg_r.at[0], other_core)

    ACC[...] = jnp.zeros_like(ACC)
    h0a.forward()
    h1a.forward()
    h0a.finish()
    h0b.start()
    h1a.finish()
    h1b.start()

    own_wo.wait()
    send_wo.wait_recv()

    def project_z(zz):
        rows = H[zz, :, :, 0:2048].reshape(128, 2048)
        for n in range(2):
            ACC[n, zz] += dot_t(rows, WO[n, :, 0:2048]).reshape(4, 32, 224)

    def project_y(yy):
        rows = H[:, yy, :, 2048:4096].reshape(128, 2048)
        for n in range(2):
            ACC[n, :, yy] += dot_t(rows, WO[n, :, 2048:4096]).reshape(4, 32, 224)

    def project(d):
        project_z((z + d) % 4)
        project_y((y + d) % 4)

    project(0)
    h0b.forward()
    h1b.forward()
    project(1)
    project(3)
    h0b.finish()
    h1b.finish()
    project(2)

    for r in range(2):
        for h in range(2):
            PS[r * 2 + h] = ACC[h, :, :, r * 16 : r * 16 + 16, :].astype(BF16)
    cross = []
    for d in (2, 1, 3):
        xx = (x + d) % 4
        cross.append(go(rcopy(PS.at[xx], RX.at[x], bx_s.at[d - 1], bx_r.at[d - 1], at(xx=xx))))
    for c in cross:
        c.wait_recv()
    total = PS[x].astype(F32)
    for d in range(1, 4):
        total += RX[(x + d) % 4].astype(F32)
    SS[...] = total.astype(BF16)
    plane = []
    for d in range(1, 16):
        q = (p + d) % 16
        plane.append(go(rcopy(SS.at[q // 4, q % 4], RY.at[p], by_s.at[d - 1], by_r.at[d - 1], at(zz=q // 4, yy=q % 4))))
    RY[p] = SS[z, y]
    for c in plane:
        c.wait_recv()

    RF[...] = RY[...].astype(F32) + hid_ref[...].astype(F32)
    res = jnp.concatenate([RF[i] for i in range(16)], axis=1)
    scaled = res * gain_ref[...]
    lane = lax.broadcasted_iota(jnp.int32, (16, 128), 1)
    square = jnp.sum(res * res, axis=1, keepdims=True)
    note = dot(scaled.astype(BF16), router_ref[...])
    MS[...] = jnp.where(lane == 32, square, note)
    msg = go(rcopy(MS, MR, m_s.at[0], m_r.at[0], at(xx=x + 1 - 2 * sec)))
    to_out = []
    for d in range(1, 4):
        xx = (x + d) % 4
        s = (xx % 2) * 2 + xx // 2
        to_out.append(go(rcopy(RF.at[pl.ds(s * 4, 4)], RL.at[x], rl_s.at[d - 1], rl_r.at[d - 1], at(xx=xx))))
    RL[x] = RF[pl.ds((sec * 2 + head) * 4, 4)]
    msg.wait_recv()
    both = MS[...] + MR[...]
    mean_square = jnp.sum(jnp.where(lane == 32, both, 0.0), axis=1, keepdims=True) / (2 * HALF)
    inv = lax.rsqrt(mean_square + norm_epsilon)
    X[z, y, head, sec, :, 0:HALF] = (scaled * inv).astype(BF16)
    affinity = jax.nn.sigmoid(both * inv)
    expert = lane % 64
    hit = jnp.zeros((16, 128), F32)
    for k in range(TOP):
        hit += jnp.where((ids_ref[:, k : k + 1] == expert) & (expert < 32), 1.0, 0.0)
    picked = jnp.where(hit > 0.0, affinity, 0.0)
    gate = route_scale * picked / jnp.sum(jnp.where(lane < 64, picked, 0.0), axis=1, keepdims=True)
    top = gate.astype(BF16).astype(F32)
    X[z, y, head, sec, :, HALF:] = jnp.where(lane < 64, top, gate - top).astype(BF16)

    def row_ring(k, part, dim, done):
        c0, c1, c2 = PARTS[part]

        def view(a, b):
            def block(i):
                zi = i if dim == "z" else slice(None) if "z" in done else z
                yi = i if dim == "y" else slice(None) if "y" in done else y
                if "x" in done:
                    return X.at[zi, yi, :, :, :, pl.ds(a, b - a)]
                xi = i if dim == "x" else x
                return X.at[zi, yi, xi // 2, xi % 2, :, pl.ds(a, b - a)]

            return block

        return Ring(k, dim, view(c0, c2), view(c0, c1), view(c1, c2))

    orders = ("xyz", "yzx", "zxy")
    stages = [
        [row_ring(4 + st * 3 + part, part, orders[part][st], orders[part][:st]) for part in range(3)] for st in range(3)
    ]
    GU[...] = jnp.zeros_like(GU)
    for st in range(3):
        if st > 0:
            for ring, before in zip(stages[st], stages[st - 1]):
                before.finish()
                ring.start()
        else:
            for ring in stages[st]:
                ring.start()
        if st < 2:
            for ring in stages[st]:
                ring.forward()

    for c in send_wd:
        c.wait_recv()
    own_wd.wait()

    pass_on = []
    for i in range(4):
        pass_on.append(go(rcopy(WD.at[i, core], WD.at[i, core], wf_s.at[i], wf_r.at[i], other_core)))
    pltpu.make_async_copy(WGU.at[core], WGU.at[core], loc.at[2]).wait()
    wgu_all.wait_recv()

    def cols(part):
        return PARTS[part][0], min(PARTS[part][2], HALF)

    def experts_z(zz):
        a, b = cols(0)
        for h in range(2):
            rows = X[zz, :, :, h, :, a:b].reshape(128, b - a)
            for e in range(2):
                GU[e, zz] += dot(rows, WGU[e, h, a:b]).reshape(4, 2, 16, 512)

    def experts_x(xx):
        a, b = cols(1)
        r, h = xx // 2, xx % 2
        rows = X[:, :, r, h, :, a:b].reshape(256, b - a)
        for e in range(2):
            GU[e, :, :, r] += dot(rows, WGU[e, h, a:b]).reshape(4, 4, 16, 512)

    def experts_y(yy):
        a, b = cols(2)
        for h in range(2):
            rows = X[:, yy, :, h, :, a:b].reshape(128, b - a)
            for e in range(2):
                GU[e, :, yy] += dot(rows, WGU[e, h, a:b]).reshape(4, 2, 16, 512)

    def experts(d):
        experts_z((z + d) % 4)
        experts_x((x + d) % 4)
        experts_y((y + d) % 4)

    experts(0)
    for ring in stages[2]:
        ring.forward()
    experts(1)
    experts(3)
    for ring in stages[2]:
        ring.finish()
    experts(2)

    def activate(zz, carry):
        gates = X[zz, :, :, 0, :, HALF:].reshape(128, 128).astype(F32)
        wide = lax.broadcasted_iota(jnp.int32, (128, 128), 1) % 64
        for e in range(2):
            weight = jnp.sum(jnp.where(wide == p * 2 + e, gates, 0.0), axis=1, keepdims=True)
            gu = GU[e, zz].reshape(128, 512)
            act = jax.nn.silu(gu[:, :256]) * gu[:, 256:] * weight
            A[x, zz, :, :, e * 256 : e * 256 + 256] = act.astype(BF16).reshape(4, 32, 256)
        return carry

    lax.fori_loop(0, 4, activate, 0)

    act_ring = Ring(13, "x", lambda i: A.at[i], lambda i: A.at[i, pl.ds(0, 2)], lambda i: A.at[i, pl.ds(2, 2)])
    act_ring.start()
    act_ring.forward()
    for c in pass_on:
        c.wait_recv()
    act_ring.finish()

    def down_y(yy):
        acc = jnp.zeros((128, 896), F32)
        for i in range(4):
            acc += dot(A[i, :, yy].reshape(128, 512), WD[i, :, :, 0:896].reshape(512, 896))
        return acc.reshape(4, 32, 896)

    def down_z(zz):
        acc = jnp.zeros((128, 896), F32)
        for i in range(4):
            acc += dot(A[i, zz].reshape(128, 512), WD[i, :, :, 896:1792].reshape(512, 896))
        return acc.reshape(4, 32, 896)

    first = []
    for j, d in enumerate((2, 1, 3)):
        yy, zz = (y + d) % 4, (z + d) % 4
        Y0[j] = down_y(yy).astype(BF16)
        first.append(go(rcopy(Y0.at[j], R0.at[j], y1_s.at[0, j], y1_r.at[0, j], at(yy=yy))))
        Y1[j] = down_z(zz).astype(BF16)
        first.append(go(rcopy(Y1.at[j], R1.at[j], y1_s.at[1, j], y1_r.at[1, j], at(zz=zz))))
    OWN[0] = down_y(y)
    OWN[1] = down_z(z)
    for c in first:
        c.wait_recv()
    for i in range(4):
        t0 = OWN[0, i]
        t1 = OWN[1, i]
        for j in range(3):
            t0 += R0[j, i].astype(F32)
            t1 += R1[j, i].astype(F32)
        OWN[0, i] = t0
        OWN[1, i] = t1
        T0[i] = t0.astype(BF16)
        T1[i] = t1.astype(BF16)
    second = []
    for j, d in enumerate((2, 1, 3)):
        yy, zz = (y + d) % 4, (z + d) % 4
        second.append(go(rcopy(T0.at[zz], Q0.at[j], y2_s.at[0, j], y2_r.at[0, j], at(zz=zz))))
        second.append(go(rcopy(T1.at[yy], Q1.at[j], y2_s.at[1, j], y2_r.at[1, j], at(yy=yy))))
    for c in to_out:
        c.wait_recv()
    for c in second:
        c.wait_recv()
    m0 = OWN[0, z]
    m1 = OWN[1, y]
    for j in range(3):
        m0 += Q0[j].astype(F32)
        m1 += Q1[j].astype(F32)
    for r in range(2):
        rows = slice(r * 16, r * 16 + 16)
        low = jnp.concatenate([RL[r * 2 + h, i] for i in range(2) for h in range(2)], axis=1)
        high = jnp.concatenate([RL[r * 2 + h, i] for i in range(2, 4) for h in range(2)], axis=1)
        out_ref[rows, 0:896] = (low + m0[rows]).astype(BF16)
        out_ref[rows, 896:1792] = (high + m1[rows]).astype(BF16)

    for c in sends:
        c.wait_send()
    wgu_all.wait_send()


def body(
    hidden_in, queries, latent_cache, new_latent, cache_lengths, value_up, out_proj, norm_gain, router, expert_ids,
    w_gate_up, w_down,
):
    row_count = hidden_in.shape[0]
    model_width = hidden_in.shape[1]
    latent_width = value_up.shape[1]
    cache_depth = latent_cache.shape[1]
    sec = lax.axis_index("sec")
    head = lax.axis_index("head")
    score_scale = QKD ** (-0.5)
    scores = jnp.einsum("thk,tjk->thj", queries, latent_cache, preferred_element_type=F32) * score_scale
    own_score = jnp.einsum("thk,tk->th", queries, new_latent, preferred_element_type=F32) * score_scale
    positions = lax.broadcasted_iota(jnp.int32, (1, 1, cache_depth), 2)
    in_cache = positions < cache_lengths[:, None, None]
    scores = jnp.where(in_cache, scores, -jnp.inf)
    top_score = jnp.maximum(jnp.max(scores, axis=2), own_score)
    cache_exp = jnp.exp(scores - top_score[:, :, None])
    own_exp = jnp.exp(own_score - top_score)
    softmax_sum = jnp.sum(cache_exp, axis=2) + own_exp
    cache_weights = (cache_exp / softmax_sum[:, :, None]).astype(BF16)
    own_weights = (own_exp / softmax_sum).astype(BF16)
    latent_out = jnp.einsum(
        "thj,tjc->thc", cache_weights, latent_cache[:, :, :latent_width], preferred_element_type=F32
    )
    latent_out = latent_out + own_weights.astype(F32)[:, :, None] * new_latent[:, None, :latent_width].astype(F32)
    latent_out = latent_out.astype(BF16)
    head_out = jnp.einsum("thc,hcd->thd", latent_out, value_up, preferred_element_type=F32).astype(BF16)
    head_out = head_out.reshape(row_count, -1)

    hid = lax.dynamic_index_in_dim(hidden_in.reshape(2, 16, 16, 2, 224), head, 0, False)
    hid = lax.dynamic_index_in_dim(hid, sec, 2, False).transpose(1, 0, 2)
    gain = lax.dynamic_index_in_dim(norm_gain.reshape(16, 2, 224), sec, 1, False).reshape(1, HALF)
    rout = lax.dynamic_index_in_dim(router.reshape(16, 2, 224, 32), sec, 1, False).reshape(HALF, 32)
    blank = jnp.zeros((HALF, 32), BF16)
    rout = jnp.concatenate([rout, blank, rout, blank], axis=1)
    ids = lax.dynamic_slice_in_dim(expert_ids, head * 16, 16, 0)
    wgu = w_gate_up[0].reshape(16, 2, 224, 512)

    any_spec = pl.BlockSpec(memory_space=pl.ANY)
    vmem = pl.BlockSpec(memory_space=pltpu.VMEM)
    dma = pltpu.SemaphoreType.DMA
    return pl.pallas_call(
        layer_kernel,
        out_shape=jax.ShapeDtypeStruct((32, 1792), BF16),
        in_specs=[any_spec] * 4 + [vmem] * 4,
        out_specs=vmem,
        scratch_shapes=[
            pltpu.VMEM((4, 4, 32, 4096), BF16),
            pltpu.VMEM((2, 224, 4096), BF16),
            pltpu.VMEM((2, 4, 4, 32, 224), F32),
            pltpu.VMEM((4, 4, 4, 16, 224), BF16),
            pltpu.VMEM((4, 4, 4, 16, 224), BF16),
            pltpu.VMEM((4, 4, 16, 224), BF16),
            pltpu.VMEM((16, 16, 224), BF16),
            pltpu.VMEM((16, 128), F32),
            pltpu.VMEM((16, 128), F32),
            pltpu.VMEM((16, 16, 224), F32),
            pltpu.VMEM((4, 4, 16, 224), F32),
            pltpu.VMEM((4, 4, 2, 2, 16, 3712), BF16),
            pltpu.VMEM((2, 2, HALF, 512), BF16),
            pltpu.VMEM((2, 4, 4, 2, 16, 512), F32),
            pltpu.VMEM((4, 2, 256, 1792), BF16),
            pltpu.VMEM((4, 4, 4, 32, 512), BF16),
            pltpu.VMEM((3, 4, 32, 896), BF16),
            pltpu.VMEM((3, 4, 32, 896), BF16),
            pltpu.VMEM((2, 4, 32, 896), F32),
            pltpu.VMEM((3, 4, 32, 896), BF16),
            pltpu.VMEM((3, 4, 32, 896), BF16),
            pltpu.VMEM((4, 32, 896), BF16),
            pltpu.VMEM((4, 32, 896), BF16),
            pltpu.VMEM((3, 32, 896), BF16),
            pltpu.VMEM((3, 32, 896), BF16),
            dma((14, 4)),
            dma((14, 4)),
            dma((3,)),
            dma((3,)),
            dma((15,)),
            dma((15,)),
            dma((1,)),
            dma((1,)),
            dma((3,)),
            dma((3,)),
            dma((1,)),
            dma((1,)),
            dma((1,)),
            dma((1,)),
            dma((3,)),
            dma((3,)),
            dma((4,)),
            dma((4,)),
            dma((2, 3)),
            dma((2, 3)),
            dma((2, 3)),
            dma((2, 3)),
            dma((4,)),
        ],
        compiler_params=pltpu.CompilerParams(
            collective_id=0, has_side_effects=True, vmem_limit_bytes=66_000_000
        ),
        name="layer",
    )(head_out, out_proj.T, wgu, w_down[0], hid, gain, rout, ids)


def solution(mesh):
    in_specs = (
        P("batch", None),
        P("batch", ("sec", "head"), None),
        P("batch", None, None),
        P("batch", None),
        P("batch"),
        P(("sec", "head"), None, None),
        P(("sec", "head"), "batch"),
        P(),
        P(),
        P("batch", None),
        P("batch", None, None, ("sec", "head")),
        P("batch", ("sec", "head"), None),
    )
    out_specs = P("batch", ("sec", "head"))
    return jax.shard_map(body, mesh=mesh, in_specs=in_specs, out_specs=out_specs, check_vma=False)
```

```python
import jax
import jax.numpy as jnp
from jax import lax
from jax.experimental import pallas as pl
from jax.experimental.pallas import tpu as pltpu
from jax.sharding import PartitionSpec as P

QKD = 192
TOP = 8
norm_epsilon = 1e-06
route_scale = 2.5

BF16, F32 = jnp.bfloat16, jnp.float32
MESH = pl.DeviceIdType.MESH
PARTS = ((0, 640, 1280), (1280, 1920, 2560), (2560, 3200, 3712))
HALF = 3584
GROUP = 8


def dot(a, b):
    return lax.dot_general(a, b, (((1,), (0,)), ((), ())), preferred_element_type=F32)


def dot_t(a, b):
    return lax.dot_general(a, b, (((1,), (1,)), ((), ())), preferred_element_type=F32)


def layer_kernel(
    q_hbm, cache_hbm, vu_hbm, wo_hbm, wgu_hbm, wd_hbm, new_ref, hidden_ref, gain_ref, router_ref, ids_ref, len_ref,
    out_ref,
    CA, Q, NEW, L, VU, RAW, PERM, HID, GAIN, ROUT, HIT,
    H, WO, ACC, PS, RX, SS, RY, MS, MR, RF, RL, X, WGU, GU, WD, A, Y0, Y1, R0, R1, T0, T1, Q0, Q1, O0,
    ring_s, ring_r, bx_s, bx_r, by_s, by_r, m_s, m_r, rl_s, rl_r, wo_s, wo_r, wg_s, wg_r, wd_s, wd_r, wf_s, wf_r,
    y0_s, y0_r, y1_s, y1_r, y2_s, y2_r, loc, ca_sem, raw_sem,
):
    sec = lax.axis_index("sec")
    head = lax.axis_index("head")
    batch = lax.axis_index("batch")
    core = batch % 2
    y = (batch // 2) % 4
    z = batch // 8
    x = head * 2 + sec
    p = z * 4 + y

    def at(zz=None, yy=None, cc=None, xx=None):
        zz = z if zz is None else zz
        yy = y if yy is None else yy
        cc = core if cc is None else cc
        xx = x if xx is None else xx
        return (xx % 2, zz * 8 + yy * 2 + cc, xx // 2)

    barrier = pltpu.get_barrier_semaphore()

    def greet(to):
        pl.semaphore_signal(barrier, inc=1, device_id=to, device_id_type=MESH)

    greet(at(cc=1 - core))
    for d in range(1, 4):
        greet(at(xx=(x + d) % 4))
    for d in range(1, 16):
        q = (p + d) % 16
        greet(at(zz=q // 4, yy=q % 4))

    def rcopy(src, dst, send, recv, to):
        return pltpu.make_async_remote_copy(
            src_ref=src, dst_ref=dst, send_sem=send, recv_sem=recv, device_id=to, device_id_type=MESH
        )

    def lcopy(src, dst, k):
        return pltpu.make_async_copy(src, dst, loc.at[k])

    sends = []

    def go(copy):
        copy.start()
        sends.append(copy)
        return copy

    def cache_copy(g, slot):
        return pltpu.make_async_copy(
            cache_hbm.at[pl.ds(g * GROUP, GROUP)], CA.at[slot, :, pl.ds(0, 192)], ca_sem.at[slot]
        )

    def raw_copy(i, slot):
        rows = pl.ds(pl.multiple_of(i * 3584, 128), 3584)
        return pltpu.make_async_copy(wgu_hbm.at[rows], RAW.at[slot], raw_sem.at[slot])

    own_q = lcopy(q_hbm, Q, 0)
    own_q.start()
    cache_copy(0, 0).start()
    cache_copy(1, 1).start()
    own_vu = lcopy(vu_hbm, VU, 2)
    own_vu.start()
    own_wo = lcopy(wo_hbm, WO.at[core], 1)
    own_wo.start()
    raw_copy(0, 0).start()
    raw_copy(1, 1).start()

    def wd_cols(xx):
        s = (xx % 2) * 2 + xx // 2
        return wd_hbm.at[:, pl.ds(pl.multiple_of(s * 1792, 128), 1792)]

    own_wd = lcopy(wd_cols(x), WD.at[x, core], 3)
    own_wd.start()
    NEW[...] = new_ref[...].astype(F32)
    own_q.wait()
    pl.semaphore_wait(barrier, 19)

    other_core = at(cc=1 - core)
    send_wo = go(rcopy(wo_hbm, WO.at[core], wo_s.at[0], wo_r.at[0], other_core))
    send_wd = []
    for d in (1, 3, 2):
        xx = (x + d) % 4
        send_wd.append(go(rcopy(wd_cols(xx), WD.at[x, core], wd_s.at[d - 1], wd_r.at[d - 1], at(xx=xx))))

    own_row = lax.broadcasted_iota(jnp.int32, (16, 576), 0) == 0
    column = lax.broadcasted_iota(jnp.int32, (GROUP * 32, 208), 1)

    def attend(g, carry):
        slot = g % 2
        cache_copy(g, slot).wait()
        news = [NEW[pl.ds(g * GROUP + i, 1), :] for i in range(GROUP)]
        for i in range(GROUP):
            CA[slot, i, 192:208, :] = jnp.where(own_row, news[i], 0.0).astype(BF16)
        lengths = jnp.concatenate([jnp.full((32, 1), len_ref[g * GROUP + i], jnp.int32) for i in range(GROUP)], axis=0)
        scores = jnp.concatenate([dot_t(Q[g * GROUP + i], CA[slot, i]) for i in range(GROUP)], axis=0) * (QKD**-0.5)
        scores = jnp.where((column < lengths) | (column == 192), scores, -jnp.inf)
        weights = jnp.exp(scores - jnp.max(scores, axis=1, keepdims=True))
        weights = (weights / jnp.sum(weights, axis=1, keepdims=True)).astype(BF16)
        for i in range(GROUP):
            rows = pl.ds(pl.multiple_of((g * GROUP + i) * 32, 32), 32)
            latent = dot(weights[i * 32 : i * 32 + 32], CA[slot, i, :, 0:512])
            for c in range(4):
                L[c, rows, :] = latent[:, c * 128 : c * 128 + 128]

        @pl.when(g + 2 < 32 // GROUP)
        def _():
            cache_copy(g + 2, slot).start()

        return carry

    lax.fori_loop(0, 32 // GROUP, attend, 0)
    own_vu.wait()

    def head_values(h, carry):
        latent = jnp.concatenate([L[c, pl.ds(h, 32, stride=32), :] for c in range(4)], axis=1).astype(BF16)
        H[z, y, :, pl.ds(pl.multiple_of(h * 128, 128), 128)] = dot(latent, VU[h]).astype(BF16)
        return carry

    dims = {"z": z, "y": y, "x": x}

    def neighbour(dim, d):
        i = (dims[dim] + d) % 4
        return at(zz=i) if dim == "z" else at(yy=i) if dim == "y" else at(xx=i)

    class Ring:
        def __init__(self, k, dim, full, low, high):
            self.k, self.dim, self.full, self.low, self.high = k, dim, full, low, high

        def copy(self, part, i, d, j):
            i = (dims[self.dim] + i) % 4
            return rcopy(part(i), part(i), ring_s.at[self.k, j], ring_r.at[self.k, j], neighbour(self.dim, d))

        def start(self):
            self.up = go(self.copy(self.full, 0, 1, 0))
            self.down = go(self.copy(self.full, 0, 3, 1))

        def forward(self):
            self.up.wait_recv()
            self.far_up = go(self.copy(self.low, 3, 1, 2))
            self.down.wait_recv()
            self.far_down = go(self.copy(self.high, 1, 3, 3))

        def finish(self):
            self.far_up.wait_recv()
            self.far_down.wait_recv()

    def head_ring(k, dim, half, other_full):
        def view(rows):
            def part(i):
                cols = pl.ds(half * 2048, 2048)
                if dim == "z":
                    return H.at[i, :, rows, cols] if other_full else H.at[i, y, rows, cols]
                return H.at[:, i, rows, cols] if other_full else H.at[z, i, rows, cols]

            return part

        return Ring(k, dim, view(pl.ds(0, 32)), view(pl.ds(0, 16)), view(pl.ds(16, 16)))

    h0a, h0b = head_ring(0, "y", 0, False), head_ring(1, "z", 0, True)
    h1a, h1b = head_ring(2, "z", 1, False), head_ring(3, "y", 1, True)

    lax.fori_loop(0, 16, head_values, 0)
    h0a.start()
    lax.fori_loop(16, 32, head_values, 0)
    h1a.start()

    spread_row = lax.broadcasted_iota(jnp.int32, (256, 256), 0)
    spread_col = lax.broadcasted_iota(jnp.int32, (256, 256), 1)
    PERM[...] = jnp.where(spread_col == (spread_row % 64) * 4 + spread_row // 64, 1.0, 0.0).astype(BF16)

    def separate(i, carry):
        slot = i % 2
        raw_copy(i, slot).wait()
        for b in range(0, 14, 2):
            pair = jnp.concatenate([RAW[slot, b * 256 : b * 256 + 256], RAW[slot, b * 256 + 256 : b * 256 + 512]], axis=1)
            moved = dot(PERM[...], pair).astype(BF16)
            for j in range(2):
                for u in range(2):
                    k = (b + j) * 64 + u * 32
                    h, row = (k // 224) % 2, k // 448 * 224 + k % 224
                    row = pl.multiple_of(i * 448 + row, 32)
                    for q in range(4):
                        to = q % 2 * 256 + q // 2 * 128
                        a = q * 64 + u * 32
                        WGU[core, h, pl.ds(row, 32), to : to + 128] = moved[a : a + 32, j * 128 : j * 128 + 128]

        @pl.when(i + 2 < 8)
        def _():
            raw_copy(i + 2, slot).start()

        return carry

    def far_wgu(i, h):
        block = WGU.at[core, h, pl.ds(i * 448, 448)]
        return rcopy(block, block, wg_s.at[0], wg_r.at[0], other_core)

    wgu_all = rcopy(WGU.at[core], WGU.at[core], wg_s.at[0], wg_r.at[0], other_core)

    def pieces(v):
        return [jnp.where(sec == 0, v[:, i * 448 : i * 448 + 224], v[:, i * 448 + 224 : i * 448 + 448]) for i in range(16)]

    def pack_inputs():
        for i, piece in enumerate(pieces(hidden_ref[pl.ds(pl.multiple_of(head * 16, 16), 16), :].astype(F32))):
            HID[i] = piece
        GAIN[...] = jnp.concatenate(pieces(gain_ref[...]), axis=1)
        ROUT[0:32, :] = jnp.concatenate(pieces(router_ref[...].astype(F32)), axis=1).astype(BF16)
        ROUT[32:128, :] = jnp.zeros((96, HALF), BF16)
        expert = lax.broadcasted_iota(jnp.int32, (128, 32), 0)
        hit = jnp.zeros((128, 32), F32)
        for k in range(TOP):
            hit += jnp.where(ids_ref[k : k + 1, :] == expert, 1.0, 0.0)
        mine = lax.broadcasted_iota(jnp.int32, (16, 32), 1) == lax.broadcasted_iota(jnp.int32, (16, 32), 0) + head * 16
        HIT[...] = dot_t(jnp.where(mine, 1.0, 0.0).astype(BF16), hit.astype(BF16))

    ACC[...] = jnp.zeros_like(ACC)
    lax.fori_loop(0, 2, separate, 0)
    h0a.forward()
    h1a.forward()
    lax.fori_loop(2, 4, separate, 0)
    h0a.finish()
    h0b.start()
    h1a.finish()
    h1b.start()
    for i in range(4):
        for h in range(2):
            far_wgu(i, h).start()
    lax.fori_loop(4, 8, separate, 0)
    pack_inputs()
    for i in range(4, 8):
        for h in range(2):
            far_wgu(i, h).start()

    own_wo.wait()
    send_wo.wait_recv()

    def project_z(zz):
        rows = H[zz, :, :, 0:2048].reshape(128, 2048)
        for n in range(2):
            ACC[n, zz] += dot_t(rows, WO[n, :, 0:2048]).reshape(4, 32, 224)

    def project_y(yy):
        rows = H[:, yy, :, 2048:4096].reshape(128, 2048)
        for n in range(2):
            ACC[n, :, yy] += dot_t(rows, WO[n, :, 2048:4096]).reshape(4, 32, 224)

    def project(d):
        project_z((z + d) % 4)
        project_y((y + d) % 4)

    project(0)
    h0b.forward()
    h1b.forward()
    project(1)
    project(3)
    h0b.finish()
    h1b.finish()
    project(2)

    for r in range(2):
        for h in range(2):
            PS[r * 2 + h] = ACC[h, :, :, r * 16 : r * 16 + 16, :].astype(BF16)
    cross = []
    for d in (2, 1, 3):
        xx = (x + d) % 4
        cross.append(go(rcopy(PS.at[xx], RX.at[x], bx_s.at[d - 1], bx_r.at[d - 1], at(xx=xx))))
    for c in cross:
        c.wait_recv()
    total = PS[x].astype(F32)
    for d in range(1, 4):
        total += RX[(x + d) % 4].astype(F32)
    SS[...] = total.astype(BF16)
    plane = []
    for d in range(1, 16):
        q = (p + d) % 16
        plane.append(go(rcopy(SS.at[q // 4, q % 4], RY.at[p], by_s.at[d - 1], by_r.at[d - 1], at(zz=q // 4, yy=q % 4))))
    RY[p] = SS[z, y]
    for c in plane:
        c.wait_recv()

    RF[...] = RY[...].astype(F32) + HID[...]
    res = jnp.concatenate([RF[i] for i in range(16)], axis=1)
    scaled = res * GAIN[...]
    lane = lax.broadcasted_iota(jnp.int32, (16, 128), 1)
    square = jnp.sum(res * res, axis=1, keepdims=True)
    note = dot_t(scaled.astype(BF16), ROUT[...])
    MS[...] = jnp.where(lane == 32, square, note)
    msg = go(rcopy(MS, MR, m_s.at[0], m_r.at[0], at(xx=x + 1 - 2 * sec)))
    to_out = []
    for d in range(1, 4):
        xx = (x + d) % 4
        s = (xx % 2) * 2 + xx // 2
        to_out.append(go(rcopy(RF.at[pl.ds(s * 4, 4)], RL.at[x], rl_s.at[d - 1], rl_r.at[d - 1], at(xx=xx))))
    RL[x] = RF[pl.ds((sec * 2 + head) * 4, 4)]
    msg.wait_recv()
    both = MS[...] + MR[...]
    mean_square = jnp.sum(jnp.where(lane == 32, both, 0.0), axis=1, keepdims=True) / (2 * HALF)
    inv = lax.rsqrt(mean_square + norm_epsilon)
    X[z, y, head, sec, :, 0:HALF] = (scaled * inv).astype(BF16)
    affinity = jax.nn.sigmoid(both * inv)
    picked = jnp.where(HIT[...] > 0.0, affinity, 0.0)
    gate = route_scale * picked / jnp.sum(picked, axis=1, keepdims=True)
    top = gate.astype(BF16).astype(F32)
    X[z, y, head, sec, :, HALF:] = (top + pltpu.roll(gate - top, 64, 1)).astype(BF16)

    def row_ring(k, part, dim, done):
        c0, c1, c2 = PARTS[part]

        def view(a, b):
            def block(i):
                zi = i if dim == "z" else slice(None) if "z" in done else z
                yi = i if dim == "y" else slice(None) if "y" in done else y
                if "x" in done:
                    return X.at[zi, yi, :, :, :, pl.ds(a, b - a)]
                xi = i if dim == "x" else x
                return X.at[zi, yi, xi // 2, xi % 2, :, pl.ds(a, b - a)]

            return block

        return Ring(k, dim, view(c0, c2), view(c0, c1), view(c1, c2))

    orders = ("xyz", "yzx", "zxy")
    stages = [
        [row_ring(4 + st * 3 + part, part, orders[part][st], orders[part][:st]) for part in range(3)] for st in range(3)
    ]
    GU[...] = jnp.zeros_like(GU)
    for st in range(3):
        if st > 0:
            for ring, before in zip(stages[st], stages[st - 1]):
                before.finish()
                ring.start()
        else:
            for ring in stages[st]:
                ring.start()
        if st < 2:
            for ring in stages[st]:
                ring.forward()

    for c in send_wd:
        c.wait_recv()
    own_wd.wait()

    pass_on = []
    for i in range(4):
        pass_on.append(go(rcopy(WD.at[i, core], WD.at[i, core], wf_s.at[i], wf_r.at[i], other_core)))
    wgu_all.wait_recv()

    def cols(part):
        return PARTS[part][0], min(PARTS[part][2], HALF)

    def experts_z(zz):
        a, b = cols(0)
        for h in range(2):
            rows = X[zz, :, :, h, :, a:b].reshape(128, b - a)
            for e in range(2):
                GU[e, zz] += dot(rows, WGU[e, h, a:b]).reshape(4, 2, 16, 512)

    def experts_x(xx):
        a, b = cols(1)
        r, h = xx // 2, xx % 2
        rows = X[:, :, r, h, :, a:b].reshape(256, b - a)
        for e in range(2):
            GU[e, :, :, r] += dot(rows, WGU[e, h, a:b]).reshape(4, 4, 16, 512)

    def experts_y(yy):
        a, b = cols(2)
        for h in range(2):
            rows = X[:, yy, :, h, :, a:b].reshape(128, b - a)
            for e in range(2):
                GU[e, :, yy] += dot(rows, WGU[e, h, a:b]).reshape(4, 2, 16, 512)

    def experts(d):
        experts_z((z + d) % 4)
        experts_x((x + d) % 4)
        experts_y((y + d) % 4)

    experts(0)
    for ring in stages[2]:
        ring.forward()
    experts(1)
    experts(3)
    for ring in stages[2]:
        ring.finish()
    experts(2)

    wide = lax.broadcasted_iota(jnp.int32, (128, 128), 1) % 64

    def activate(zz):
        gates = X[zz, :, :, 0, :, HALF:].reshape(128, 128).astype(F32)
        for e in range(2):
            weight = jnp.sum(jnp.where(wide == p * 2 + e, gates, 0.0), axis=1, keepdims=True)
            gu = GU[e, zz].reshape(128, 512)
            act = jax.nn.silu(gu[:, :256]) * gu[:, 256:] * weight
            A[x, zz, :, :, e * 256 : e * 256 + 256] = act.astype(BF16).reshape(4, 32, 256)

    def act_ring(j):
        zz = (z + order[j]) % 4
        return Ring(
            13 + j, "x", lambda i: A.at[i, zz], lambda i: A.at[i, zz, pl.ds(0, 2)], lambda i: A.at[i, zz, pl.ds(2, 2)]
        )

    order = (2, 1, 3, 0)
    acts = [act_ring(j) for j in range(4)]
    over_y, over_z, last_z, last_y = [], [], [], []

    def down(j):
        zz = (z + order[j]) % 4
        for half, buf in ((1, Y1), (0, Y0)):
            acc = jnp.zeros((128, 896), F32)
            for i in range(4):
                acc += dot(A[i, zz].reshape(128, 512), WD[i, :, :, half * 896 : half * 896 + 896].reshape(512, 896))
            buf[j] = acc.reshape(4, 32, 896).astype(BF16)
            if half == 1 and j < 3:
                over_z.append(go(rcopy(Y1.at[j], R1.at[j], y1_s.at[j], y1_r.at[j], at(zz=zz))))
        group = []
        for m in range(3):
            yy = (y + order[m]) % 4
            group.append(go(rcopy(Y0.at[j, yy], R0.at[j, m], y0_s.at[j, m], y0_r.at[j, m], at(yy=yy))))
        over_y.append(group)

    def gather_y(j):
        zz = (z + order[j]) % 4
        for c in over_y[j]:
            c.wait_recv()
        acc = Y0[j, y].astype(F32)
        for m in range(3):
            acc += R0[j, m].astype(F32)
        if j < 3:
            T0[j] = acc.astype(BF16)
            last_z.append(go(rcopy(T0.at[j], Q0.at[j], y2_s.at[0, j], y2_r.at[0, j], at(zz=zz))))
        else:
            O0[...] = acc

    activate((z + order[0]) % 4)
    acts[0].start()
    activate((z + order[1]) % 4)
    acts[1].start()
    activate((z + order[2]) % 4)
    activate((z + order[3]) % 4)
    acts[0].forward()
    acts[2].start()
    for c in pass_on:
        c.wait_recv()
    acts[1].forward()
    acts[0].finish()
    acts[3].start()
    down(0)
    acts[2].forward()
    acts[1].finish()
    down(1)
    gather_y(0)
    acts[3].forward()
    acts[2].finish()
    down(2)
    gather_y(1)
    acts[3].finish()
    down(3)
    gather_y(2)
    for c in over_z:
        c.wait_recv()

    def sum_z(yy):
        acc = Y1[3, yy].astype(F32)
        for m in range(3):
            acc += R1[m, yy].astype(F32)
        return acc

    for m in range(3):
        yy = (y + order[m]) % 4
        T1[m] = sum_z(yy).astype(BF16)
        last_y.append(go(rcopy(T1.at[m], Q1.at[m], y2_s.at[1, m], y2_r.at[1, m], at(yy=yy))))
    gather_y(3)
    m0 = O0[...]
    m1 = sum_z(y)
    for c in to_out + last_z + last_y:
        c.wait_recv()
    for m in range(3):
        m0 += Q0[m].astype(F32)
        m1 += Q1[m].astype(F32)
    for r in range(2):
        rows = slice(r * 16, r * 16 + 16)
        low = jnp.concatenate([RL[r * 2 + h, i] for i in range(2) for h in range(2)], axis=1)
        high = jnp.concatenate([RL[r * 2 + h, i] for i in range(2, 4) for h in range(2)], axis=1)
        out_ref[rows, 0:896] = (low + m0[rows]).astype(BF16)
        out_ref[rows, 896:1792] = (high + m1[rows]).astype(BF16)

    for c in sends:
        c.wait_send()
    wgu_all.wait_send()


def body(
    hidden_in, queries, latent_cache, new_latent, cache_lengths, value_up, out_proj, norm_gain, router, expert_ids,
    w_gate_up, w_down,
):
    wgu = w_gate_up[0].reshape(7168, 2, 2, 128).transpose(0, 2, 1, 3).reshape(28672, 128)
    any_spec = pl.BlockSpec(memory_space=pl.ANY)
    vmem = pl.BlockSpec(memory_space=pltpu.VMEM)
    dma = pltpu.SemaphoreType.DMA
    return pl.pallas_call(
        layer_kernel,
        out_shape=jax.ShapeDtypeStruct((32, 1792), BF16),
        in_specs=[any_spec] * 6 + [vmem] * 5 + [pl.BlockSpec(memory_space=pltpu.SMEM)],
        out_specs=vmem,
        scratch_shapes=[
            pltpu.VMEM((2, GROUP, 208, 576), BF16),
            pltpu.VMEM((32, 32, 576), BF16),
            pltpu.VMEM((32, 576), F32),
            pltpu.VMEM((4, 1024, 128), F32),
            pltpu.VMEM((32, 512, 128), BF16),
            pltpu.VMEM((2, 3584, 128), BF16),
            pltpu.VMEM((256, 256), BF16),
            pltpu.VMEM((16, 16, 224), F32),
            pltpu.VMEM((1, HALF), F32),
            pltpu.VMEM((128, HALF), BF16),
            pltpu.VMEM((16, 128), F32),
            pltpu.VMEM((4, 4, 32, 4096), BF16),
            pltpu.VMEM((2, 224, 4096), BF16),
            pltpu.VMEM((2, 4, 4, 32, 224), F32),
            pltpu.VMEM((4, 4, 4, 16, 224), BF16),
            pltpu.VMEM((4, 4, 4, 16, 224), BF16),
            pltpu.VMEM((4, 4, 16, 224), BF16),
            pltpu.VMEM((16, 16, 224), BF16),
            pltpu.VMEM((16, 128), F32),
            pltpu.VMEM((16, 128), F32),
            pltpu.VMEM((16, 16, 224), F32),
            pltpu.VMEM((4, 4, 16, 224), F32),
            pltpu.VMEM((4, 4, 2, 2, 16, 3712), BF16),
            pltpu.VMEM((2, 2, HALF, 512), BF16),
            pltpu.VMEM((2, 4, 4, 2, 16, 512), F32),
            pltpu.VMEM((4, 2, 256, 1792), BF16),
            pltpu.VMEM((4, 4, 4, 32, 512), BF16),
            pltpu.VMEM((4, 4, 32, 896), BF16),
            pltpu.VMEM((4, 4, 32, 896), BF16),
            pltpu.VMEM((4, 3, 32, 896), BF16),
            pltpu.VMEM((3, 4, 32, 896), BF16),
            pltpu.VMEM((3, 32, 896), BF16),
            pltpu.VMEM((3, 32, 896), BF16),
            pltpu.VMEM((3, 32, 896), BF16),
            pltpu.VMEM((3, 32, 896), BF16),
            pltpu.VMEM((32, 896), F32),
            dma((17, 4)),
            dma((17, 4)),
            dma((3,)),
            dma((3,)),
            dma((15,)),
            dma((15,)),
            dma((1,)),
            dma((1,)),
            dma((3,)),
            dma((3,)),
            dma((1,)),
            dma((1,)),
            dma((1,)),
            dma((1,)),
            dma((3,)),
            dma((3,)),
            dma((4,)),
            dma((4,)),
            dma((4, 3)),
            dma((4, 3)),
            dma((3,)),
            dma((3,)),
            dma((2, 3)),
            dma((2, 3)),
            dma((4,)),
            dma((2,)),
            dma((2,)),
        ],
        compiler_params=pltpu.CompilerParams(
            collective_id=0, has_side_effects=True, vmem_limit_bytes=66_000_000
        ),
        name="layer",
    )(
        queries, latent_cache, value_up, out_proj.T, wgu, w_down[0], new_latent, hidden_in, norm_gain.reshape(1, -1),
        router.T, expert_ids.T, cache_lengths,
    )


def solution(mesh):
    in_specs = (
        P("batch", None),
        P("batch", ("sec", "head"), None),
        P("batch", None, None),
        P("batch", None),
        P("batch"),
        P(("sec", "head"), None, None),
        P(("sec", "head"), "batch"),
        P(),
        P(),
        P("batch", None),
        P("batch", None, None, ("sec", "head")),
        P("batch", ("sec", "head"), None),
    )
    out_specs = P("batch", ("sec", "head"))
    return jax.shard_map(body, mesh=mesh, in_specs=in_specs, out_specs=out_specs, check_vma=False)
```

```python
import jax
import jax.numpy as jnp
from jax import lax
from jax.experimental import pallas as pl
from jax.experimental.pallas import tpu as pltpu
from jax.sharding import PartitionSpec as P

QKD = 192
TOP = 8
norm_epsilon = 1e-06
route_scale = 2.5

BF16, F32 = jnp.bfloat16, jnp.float32
MESH = pl.DeviceIdType.MESH
PARTS = ((0, 640, 1280), (1280, 1920, 2560), (2560, 3200, 3712))
HALF = 3584
GROUP = 8


def dot(a, b):
    return lax.dot_general(a, b, (((1,), (0,)), ((), ())), preferred_element_type=F32)


def dot_t(a, b):
    return lax.dot_general(a, b, (((1,), (1,)), ((), ())), preferred_element_type=F32)


def layer_kernel(
    q_hbm, cache_hbm, vu_hbm, wo_hbm, wgu_hbm, wd_hbm, new_ref, hidden_ref, gain_ref, router_ref, ids_ref, len_ref,
    out_ref,
    CA, Q, NEW, L, VU, RAW, PERM, HID, GAIN, ROUT, HIT,
    H, WO, ACC, PS, RX, SS, RY, MS, MR, RF, RL, X, WGU, GU, WD, A, Y0, Y1, R0, R1, T0, T1, Q0, Q1, O0,
    ring_s, ring_r, bx_s, bx_r, by_s, by_r, m_s, m_r, rl_s, rl_r, wo_s, wo_r, wg_s, wg_r, wd_s, wd_r, wf_s, wf_r,
    y0_s, y0_r, y1_s, y1_r, y2_s, y2_r, loc, ca_sem, raw_sem,
):
    sec = lax.axis_index("sec")
    head = lax.axis_index("head")
    batch = lax.axis_index("batch")
    core = batch % 2
    y = (batch // 2) % 4
    z = batch // 8
    x = head * 2 + sec
    p = z * 4 + y

    def at(zz=None, yy=None, cc=None, xx=None):
        zz = z if zz is None else zz
        yy = y if yy is None else yy
        cc = core if cc is None else cc
        xx = x if xx is None else xx
        return (xx % 2, zz * 8 + yy * 2 + cc, xx // 2)

    barrier = pltpu.get_barrier_semaphore()

    def greet(to):
        pl.semaphore_signal(barrier, inc=1, device_id=to, device_id_type=MESH)

    greet(at(cc=1 - core))
    for d in range(1, 4):
        greet(at(xx=(x + d) % 4))
    for d in range(1, 16):
        q = (p + d) % 16
        greet(at(zz=q // 4, yy=q % 4))

    def rcopy(src, dst, send, recv, to):
        return pltpu.make_async_remote_copy(
            src_ref=src, dst_ref=dst, send_sem=send, recv_sem=recv, device_id=to, device_id_type=MESH
        )

    def lcopy(src, dst, k):
        return pltpu.make_async_copy(src, dst, loc.at[k])

    sends = []

    def go(copy):
        copy.start()
        sends.append(copy)
        return copy

    def cache_copy(g, slot):
        return pltpu.make_async_copy(
            cache_hbm.at[pl.ds(g * GROUP, GROUP)], CA.at[slot, :, pl.ds(0, 192)], ca_sem.at[slot]
        )

    def raw_copy(i, slot):
        rows = pl.ds(pl.multiple_of(i * 3584, 128), 3584)
        return pltpu.make_async_copy(wgu_hbm.at[rows], RAW.at[slot], raw_sem.at[slot])

    own_q = lcopy(q_hbm, Q, 0)
    own_q.start()
    cache_copy(0, 0).start()
    cache_copy(1, 1).start()
    own_vu = lcopy(vu_hbm, VU, 2)
    own_vu.start()
    own_wo = lcopy(wo_hbm, WO.at[core], 1)
    own_wo.start()
    raw_copy(0, 0).start()
    raw_copy(1, 1).start()

    def wd_cols(xx):
        s = (xx % 2) * 2 + xx // 2
        return wd_hbm.at[:, pl.ds(pl.multiple_of(s * 1792, 128), 1792)]

    own_wd = lcopy(wd_cols(x), WD.at[x, core], 3)
    own_wd.start()
    NEW[...] = new_ref[...].astype(F32)
    own_q.wait()
    pl.semaphore_wait(barrier, 19)

    other_core = at(cc=1 - core)
    send_wo = go(rcopy(wo_hbm, WO.at[core], wo_s.at[0], wo_r.at[0], other_core))
    send_wd = []
    for d in (1, 3, 2):
        xx = (x + d) % 4
        send_wd.append(go(rcopy(wd_cols(xx), WD.at[x, core], wd_s.at[d - 1], wd_r.at[d - 1], at(xx=xx))))

    own_row = lax.broadcasted_iota(jnp.int32, (16, 576), 0) == 0
    column = lax.broadcasted_iota(jnp.int32, (GROUP * 32, 208), 1)

    def attend(g, carry):
        slot = g % 2
        cache_copy(g, slot).wait()
        news = [NEW[pl.ds(g * GROUP + i, 1), :] for i in range(GROUP)]
        for i in range(GROUP):
            CA[slot, i, 192:208, :] = jnp.where(own_row, news[i], 0.0).astype(BF16)
        lengths = jnp.concatenate([jnp.full((32, 1), len_ref[g * GROUP + i], jnp.int32) for i in range(GROUP)], axis=0)
        scores = jnp.concatenate([dot_t(Q[g * GROUP + i], CA[slot, i]) for i in range(GROUP)], axis=0) * (QKD**-0.5)
        scores = jnp.where((column < lengths) | (column == 192), scores, -jnp.inf)
        weights = jnp.exp(scores - jnp.max(scores, axis=1, keepdims=True))
        weights = (weights / jnp.sum(weights, axis=1, keepdims=True)).astype(BF16)
        for i in range(GROUP):
            rows = pl.ds(pl.multiple_of((g * GROUP + i) * 32, 32), 32)
            latent = dot(weights[i * 32 : i * 32 + 32], CA[slot, i, :, 0:512])
            for c in range(4):
                L[c, rows, :] = latent[:, c * 128 : c * 128 + 128]

        @pl.when(g + 2 < 32 // GROUP)
        def _():
            cache_copy(g + 2, slot).start()

        return carry

    lax.fori_loop(0, 32 // GROUP, attend, 0)
    own_vu.wait()

    def head_values(h, carry):
        latent = jnp.concatenate([L[c, pl.ds(h, 32, stride=32), :] for c in range(4)], axis=1).astype(BF16)
        H[z, y, :, pl.ds(pl.multiple_of(h * 128, 128), 128)] = dot(latent, VU[h]).astype(BF16)
        return carry

    dims = {"z": z, "y": y, "x": x}

    def neighbour(dim, d):
        i = (dims[dim] + d) % 4
        return at(zz=i) if dim == "z" else at(yy=i) if dim == "y" else at(xx=i)

    class Ring:
        def __init__(self, k, dim, full, low, high):
            self.k, self.dim, self.full, self.low, self.high = k, dim, full, low, high

        def copy(self, part, i, d, j):
            i = (dims[self.dim] + i) % 4
            return rcopy(part(i), part(i), ring_s.at[self.k, j], ring_r.at[self.k, j], neighbour(self.dim, d))

        def start(self):
            self.up = go(self.copy(self.full, 0, 1, 0))
            self.down = go(self.copy(self.full, 0, 3, 1))

        def forward(self):
            self.up.wait_recv()
            self.far_up = go(self.copy(self.low, 3, 1, 2))
            self.down.wait_recv()
            self.far_down = go(self.copy(self.high, 1, 3, 3))

        def finish(self):
            self.far_up.wait_recv()
            self.far_down.wait_recv()

    def head_ring(k, dim, half, other):
        def view(rows):
            def part(i):
                cols = pl.ds(half * 2048, 2048)
                if dim == "z":
                    return H.at[i, (y + other) % 4, rows, cols]
                return H.at[(z + other) % 4, i, rows, cols]

            return part

        return Ring(k, dim, view(pl.ds(0, 32)), view(pl.ds(0, 16)), view(pl.ds(16, 16)))

    h0a, h0b = head_ring(0, "y", 0, 0), [head_ring(1 + o, "z", 0, o) for o in range(4)]
    h1a, h1b = head_ring(5, "z", 1, 0), [head_ring(6 + o, "y", 1, o) for o in range(4)]

    lax.fori_loop(0, 16, head_values, 0)
    h0a.start()
    h0b[0].start()
    lax.fori_loop(16, 32, head_values, 0)
    h1a.start()
    h1b[0].start()

    spread_row = lax.broadcasted_iota(jnp.int32, (256, 256), 0)
    spread_col = lax.broadcasted_iota(jnp.int32, (256, 256), 1)
    PERM[...] = jnp.where(spread_col == (spread_row % 64) * 4 + spread_row // 64, 1.0, 0.0).astype(BF16)

    def separate(i, carry):
        slot = i % 2
        raw_copy(i, slot).wait()
        for b in range(0, 14, 2):
            pair = jnp.concatenate([RAW[slot, b * 256 : b * 256 + 256], RAW[slot, b * 256 + 256 : b * 256 + 512]], axis=1)
            moved = dot(PERM[...], pair).astype(BF16)
            for j in range(2):
                for u in range(2):
                    k = (b + j) * 64 + u * 32
                    h, row = (k // 224) % 2, k // 448 * 224 + k % 224
                    row = pl.multiple_of(i * 448 + row, 32)
                    for q in range(4):
                        to = q % 2 * 256 + q // 2 * 128
                        a = q * 64 + u * 32
                        WGU[core, h, pl.ds(row, 32), to : to + 128] = moved[a : a + 32, j * 128 : j * 128 + 128]

        @pl.when(i + 2 < 8)
        def _():
            raw_copy(i + 2, slot).start()

        return carry

    def far_wgu(i, h):
        block = WGU.at[core, h, pl.ds(i * 448, 448)]
        return rcopy(block, block, wg_s.at[0], wg_r.at[0], other_core)

    wgu_all = rcopy(WGU.at[core], WGU.at[core], wg_s.at[0], wg_r.at[0], other_core)

    def pieces(v):
        return [jnp.where(sec == 0, v[:, i * 448 : i * 448 + 224], v[:, i * 448 + 224 : i * 448 + 448]) for i in range(16)]

    def pack_inputs():
        for i, piece in enumerate(pieces(hidden_ref[pl.ds(pl.multiple_of(head * 16, 16), 16), :].astype(F32))):
            HID[i] = piece
        GAIN[...] = jnp.concatenate(pieces(gain_ref[...]), axis=1)
        ROUT[0:32, :] = jnp.concatenate(pieces(router_ref[...].astype(F32)), axis=1).astype(BF16)
        ROUT[32:128, :] = jnp.zeros((96, HALF), BF16)
        expert = lax.broadcasted_iota(jnp.int32, (128, 32), 0)
        hit = jnp.zeros((128, 32), F32)
        for k in range(TOP):
            hit += jnp.where(ids_ref[k : k + 1, :] == expert, 1.0, 0.0)
        mine = lax.broadcasted_iota(jnp.int32, (16, 32), 1) == lax.broadcasted_iota(jnp.int32, (16, 32), 0) + head * 16
        HIT[...] = dot_t(jnp.where(mine, 1.0, 0.0).astype(BF16), hit.astype(BF16))

    ACC[...] = jnp.zeros_like(ACC)
    lax.fori_loop(0, 1, separate, 0)
    h0a.forward()
    h1a.forward()
    for o in (1, 3):
        h0b[o].start()
        h1b[o].start()
    lax.fori_loop(1, 2, separate, 0)
    h0b[0].forward()
    h1b[0].forward()
    h0a.finish()
    h0b[2].start()
    h1a.finish()
    h1b[2].start()
    lax.fori_loop(2, 4, separate, 0)
    for i in range(4):
        for h in range(2):
            far_wgu(i, h).start()
    lax.fori_loop(4, 7, separate, 0)
    for o in (1, 3):
        h0b[o].forward()
        h1b[o].forward()
    lax.fori_loop(7, 8, separate, 0)
    pack_inputs()
    for i in range(4, 8):
        for h in range(2):
            far_wgu(i, h).start()

    own_wo.wait()
    send_wo.wait_recv()

    def project_z(zz):
        rows = H[zz, :, :, 0:2048].reshape(128, 2048)
        for n in range(2):
            ACC[n, zz] += dot_t(rows, WO[n, :, 0:2048]).reshape(4, 32, 224)

    def project_y(yy):
        rows = H[:, yy, :, 2048:4096].reshape(128, 2048)
        for n in range(2):
            ACC[n, :, yy] += dot_t(rows, WO[n, :, 2048:4096]).reshape(4, 32, 224)

    def project(d):
        project_z((z + d) % 4)
        project_y((y + d) % 4)

    project(0)
    h0b[2].forward()
    h1b[2].forward()
    project(1)
    project(3)
    for o in range(4):
        h0b[o].finish()
        h1b[o].finish()
    project(2)

    for r in range(2):
        for h in range(2):
            PS[r * 2 + h] = ACC[h, :, :, r * 16 : r * 16 + 16, :].astype(BF16)
    cross = []
    for d in (2, 1, 3):
        xx = (x + d) % 4
        cross.append(go(rcopy(PS.at[xx], RX.at[x], bx_s.at[d - 1], bx_r.at[d - 1], at(xx=xx))))
    for c in cross:
        c.wait_recv()
    total = PS[x].astype(F32)
    for d in range(1, 4):
        total += RX[(x + d) % 4].astype(F32)
    SS[...] = total.astype(BF16)
    plane = []
    for d in range(1, 16):
        q = (p + d) % 16
        plane.append(go(rcopy(SS.at[q // 4, q % 4], RY.at[p], by_s.at[d - 1], by_r.at[d - 1], at(zz=q // 4, yy=q % 4))))
    RY[p] = SS[z, y]
    for c in plane:
        c.wait_recv()

    RF[...] = RY[...].astype(F32) + HID[...]
    res = jnp.concatenate([RF[i] for i in range(16)], axis=1)
    scaled = res * GAIN[...]
    lane = lax.broadcasted_iota(jnp.int32, (16, 128), 1)
    square = jnp.sum(res * res, axis=1, keepdims=True)
    note = dot_t(scaled.astype(BF16), ROUT[...])
    MS[...] = jnp.where(lane == 32, square, note)
    X[z, y, head, sec, :, 0:HALF] = scaled.astype(BF16)
    msg = go(rcopy(MS, MR, m_s.at[0], m_r.at[0], at(xx=x + 1 - 2 * sec)))
    def row_ring(k, part, dim, done, fixed):
        c0, c1, c2 = PARTS[part]

        def view(a, b):
            def block(i):
                at_dim = {}
                for d in "zyx":
                    at_dim[d] = i if d == dim else None if d in done else (dims[d] + fixed.get(d, 0)) % 4
                zi, yi, xi = (slice(None) if at_dim[d] is None else at_dim[d] for d in "zyx")
                if at_dim["x"] is None:
                    return X.at[zi, yi, :, :, :, pl.ds(a, b - a)]
                return X.at[zi, yi, xi // 2, xi % 2, :, pl.ds(a, b - a)]

            return block

        return Ring(k, dim, view(c0, c2), view(c0, c1), view(c1, c2))

    first, second, third = [], [], []
    for part, (d1, d2, d3) in enumerate(("xyz", "yzx", "zxy")):
        first.append(row_ring(10 + part, part, d1, "", {}))
        second.append(row_ring(13 + part, part, d2, d1, {}))
        third.append([row_ring(16 + part * 4 + o, part, d3, d1, {d2: o}) for o in range(4)])
    GU[...] = jnp.zeros_like(GU)
    first[0].start()
    first[1].start()

    msg.wait_recv()
    both = MS[...] + MR[...]
    mean_square = jnp.sum(jnp.where(lane == 32, both, 0.0), axis=1, keepdims=True) / (2 * HALF)
    inv = lax.rsqrt(mean_square + norm_epsilon)
    affinity = jax.nn.sigmoid(both * inv)
    picked = jnp.where(HIT[...] > 0.0, affinity, 0.0)
    gate = route_scale * picked / jnp.sum(picked, axis=1, keepdims=True)
    gate = jnp.where(lane == 32, inv, gate)
    top = gate.astype(BF16).astype(F32)
    X[z, y, head, sec, :, HALF:] = (top + pltpu.roll(gate - top, 64, 1)).astype(BF16)
    first[2].start()

    for ring in first:
        ring.forward()
    for before, ring in zip(first, second):
        before.finish()
        ring.start()
    for rings in third:
        rings[0].start()
    for ring in second:
        ring.forward()
    for rings in third:
        rings[1].start()
        rings[3].start()

    to_out = []
    for d in range(1, 4):
        xx = (x + d) % 4
        s = (xx % 2) * 2 + xx // 2
        to_out.append(go(rcopy(RF.at[pl.ds(s * 4, 4)], RL.at[x], rl_s.at[d - 1], rl_r.at[d - 1], at(xx=xx))))
    RL[x] = RF[pl.ds((sec * 2 + head) * 4, 4)]
    for rings in third:
        rings[0].forward()
    for before, rings in zip(second, third):
        before.finish()
        rings[2].start()

    for c in send_wd:
        c.wait_recv()
    own_wd.wait()

    pass_on = []
    for i in range(4):
        pass_on.append(go(rcopy(WD.at[i, core], WD.at[i, core], wf_s.at[i], wf_r.at[i], other_core)))
    wgu_all.wait_recv()

    def cols(part):
        return PARTS[part][0], min(PARTS[part][2], HALF)

    def experts_z(zz):
        a, b = cols(0)
        for h in range(2):
            rows = X[zz, :, :, h, :, a:b].reshape(128, b - a)
            for e in range(2):
                GU[e, zz] += dot(rows, WGU[e, h, a:b]).reshape(4, 2, 16, 512)

    def experts_x(xx):
        a, b = cols(1)
        r, h = xx // 2, xx % 2
        rows = X[:, :, r, h, :, a:b].reshape(256, b - a)
        for e in range(2):
            GU[e, :, :, r] += dot(rows, WGU[e, h, a:b]).reshape(4, 4, 16, 512)

    def experts_y(yy):
        a, b = cols(2)
        for h in range(2):
            rows = X[:, yy, :, h, :, a:b].reshape(128, b - a)
            for e in range(2):
                GU[e, :, yy] += dot(rows, WGU[e, h, a:b]).reshape(4, 2, 16, 512)

    def experts(d):
        experts_z((z + d) % 4)
        experts_x((x + d) % 4)
        experts_y((y + d) % 4)

    experts(0)
    for o in (1, 3, 2):
        for rings in third:
            rings[o].forward()
    experts(1)
    experts(3)
    for o in range(4):
        for rings in third:
            rings[o].finish()
    experts(2)

    wide = lax.broadcasted_iota(jnp.int32, (128, 128), 1) % 64

    def activate(zz):
        gates = X[zz, :, :, 0, :, HALF:].reshape(128, 128).astype(F32)
        inv = jnp.sum(jnp.where(wide == 32, gates, 0.0), axis=1, keepdims=True)
        for e in range(2):
            weight = jnp.sum(jnp.where(wide == p * 2 + e, gates, 0.0), axis=1, keepdims=True)
            gu = GU[e, zz].reshape(128, 512) * inv
            act = jax.nn.silu(gu[:, :256]) * gu[:, 256:] * weight
            A[x, zz, :, :, e * 256 : e * 256 + 256] = act.astype(BF16).reshape(4, 32, 256)

    def act_ring(j):
        zz = (z + order[j]) % 4
        return Ring(
            28 + j, "x", lambda i: A.at[i, zz], lambda i: A.at[i, zz, pl.ds(0, 2)], lambda i: A.at[i, zz, pl.ds(2, 2)]
        )

    order = (2, 1, 3, 0)
    acts = [act_ring(j) for j in range(4)]
    over_y, over_z, last_z, last_y = [], [], [], []

    def down(j):
        zz = (z + order[j]) % 4
        for half, buf in ((1, Y1), (0, Y0)):
            acc = jnp.zeros((128, 896), F32)
            for i in range(4):
                acc += dot(A[i, zz].reshape(128, 512), WD[i, :, :, half * 896 : half * 896 + 896].reshape(512, 896))
            buf[j] = acc.reshape(4, 32, 896).astype(BF16)
            if half == 1 and j < 3:
                over_z.append(go(rcopy(Y1.at[j], R1.at[j], y1_s.at[j], y1_r.at[j], at(zz=zz))))
        group = []
        for m in range(3):
            yy = (y + order[m]) % 4
            group.append(go(rcopy(Y0.at[j, yy], R0.at[j, m], y0_s.at[j, m], y0_r.at[j, m], at(yy=yy))))
        over_y.append(group)

    def gather_y(j):
        zz = (z + order[j]) % 4
        for c in over_y[j]:
            c.wait_recv()
        acc = Y0[j, y].astype(F32)
        for m in range(3):
            acc += R0[j, m].astype(F32)
        if j < 3:
            T0[j] = acc.astype(BF16)
            last_z.append(go(rcopy(T0.at[j], Q0.at[j], y2_s.at[0, j], y2_r.at[0, j], at(zz=zz))))
        else:
            O0[...] = acc

    activate((z + order[0]) % 4)
    acts[0].start()
    activate((z + order[1]) % 4)
    acts[1].start()
    activate((z + order[2]) % 4)
    activate((z + order[3]) % 4)
    acts[0].forward()
    acts[2].start()
    for c in pass_on:
        c.wait_recv()
    acts[1].forward()
    acts[0].finish()
    acts[3].start()
    down(0)
    acts[2].forward()
    acts[1].finish()
    down(1)
    gather_y(0)
    acts[3].forward()
    acts[2].finish()
    down(2)
    gather_y(1)
    acts[3].finish()
    down(3)
    gather_y(2)
    for c in over_z:
        c.wait_recv()

    def sum_z(yy):
        acc = Y1[3, yy].astype(F32)
        for m in range(3):
            acc += R1[m, yy].astype(F32)
        return acc

    for m in range(3):
        yy = (y + order[m]) % 4
        T1[m] = sum_z(yy).astype(BF16)
        last_y.append(go(rcopy(T1.at[m], Q1.at[m], y2_s.at[1, m], y2_r.at[1, m], at(yy=yy))))
    gather_y(3)
    m0 = O0[...]
    m1 = sum_z(y)
    for c in to_out + last_z + last_y:
        c.wait_recv()
    for m in range(3):
        m0 += Q0[m].astype(F32)
        m1 += Q1[m].astype(F32)
    for r in range(2):
        rows = slice(r * 16, r * 16 + 16)
        low = jnp.concatenate([RL[r * 2 + h, i] for i in range(2) for h in range(2)], axis=1)
        high = jnp.concatenate([RL[r * 2 + h, i] for i in range(2, 4) for h in range(2)], axis=1)
        out_ref[rows, 0:896] = (low + m0[rows]).astype(BF16)
        out_ref[rows, 896:1792] = (high + m1[rows]).astype(BF16)

    for c in sends:
        c.wait_send()
    wgu_all.wait_send()


def body(
    hidden_in, queries, latent_cache, new_latent, cache_lengths, value_up, out_proj, norm_gain, router, expert_ids,
    w_gate_up, w_down,
):
    wgu = w_gate_up[0].reshape(7168, 2, 2, 128).transpose(0, 2, 1, 3).reshape(28672, 128)
    any_spec = pl.BlockSpec(memory_space=pl.ANY)
    vmem = pl.BlockSpec(memory_space=pltpu.VMEM)
    dma = pltpu.SemaphoreType.DMA
    return pl.pallas_call(
        layer_kernel,
        out_shape=jax.ShapeDtypeStruct((32, 1792), BF16),
        in_specs=[any_spec] * 6 + [vmem] * 5 + [pl.BlockSpec(memory_space=pltpu.SMEM)],
        out_specs=vmem,
        scratch_shapes=[
            pltpu.VMEM((2, GROUP, 208, 576), BF16),
            pltpu.VMEM((32, 32, 576), BF16),
            pltpu.VMEM((32, 576), F32),
            pltpu.VMEM((4, 1024, 128), F32),
            pltpu.VMEM((32, 512, 128), BF16),
            pltpu.VMEM((2, 3584, 128), BF16),
            pltpu.VMEM((256, 256), BF16),
            pltpu.VMEM((16, 16, 224), F32),
            pltpu.VMEM((1, HALF), F32),
            pltpu.VMEM((128, HALF), BF16),
            pltpu.VMEM((16, 128), F32),
            pltpu.VMEM((4, 4, 32, 4096), BF16),
            pltpu.VMEM((2, 224, 4096), BF16),
            pltpu.VMEM((2, 4, 4, 32, 224), F32),
            pltpu.VMEM((4, 4, 4, 16, 224), BF16),
            pltpu.VMEM((4, 4, 4, 16, 224), BF16),
            pltpu.VMEM((4, 4, 16, 224), BF16),
            pltpu.VMEM((16, 16, 224), BF16),
            pltpu.VMEM((16, 128), F32),
            pltpu.VMEM((16, 128), F32),
            pltpu.VMEM((16, 16, 224), F32),
            pltpu.VMEM((4, 4, 16, 224), F32),
            pltpu.VMEM((4, 4, 2, 2, 16, 3712), BF16),
            pltpu.VMEM((2, 2, HALF, 512), BF16),
            pltpu.VMEM((2, 4, 4, 2, 16, 512), F32),
            pltpu.VMEM((4, 2, 256, 1792), BF16),
            pltpu.VMEM((4, 4, 4, 32, 512), BF16),
            pltpu.VMEM((4, 4, 32, 896), BF16),
            pltpu.VMEM((4, 4, 32, 896), BF16),
            pltpu.VMEM((4, 3, 32, 896), BF16),
            pltpu.VMEM((3, 4, 32, 896), BF16),
            pltpu.VMEM((3, 32, 896), BF16),
            pltpu.VMEM((3, 32, 896), BF16),
            pltpu.VMEM((3, 32, 896), BF16),
            pltpu.VMEM((3, 32, 896), BF16),
            pltpu.VMEM((32, 896), F32),
            dma((32, 4)),
            dma((32, 4)),
            dma((3,)),
            dma((3,)),
            dma((15,)),
            dma((15,)),
            dma((1,)),
            dma((1,)),
            dma((3,)),
            dma((3,)),
            dma((1,)),
            dma((1,)),
            dma((1,)),
            dma((1,)),
            dma((3,)),
            dma((3,)),
            dma((4,)),
            dma((4,)),
            dma((4, 3)),
            dma((4, 3)),
            dma((3,)),
            dma((3,)),
            dma((2, 3)),
            dma((2, 3)),
            dma((4,)),
            dma((2,)),
            dma((2,)),
        ],
        compiler_params=pltpu.CompilerParams(
            collective_id=0, has_side_effects=True, vmem_limit_bytes=66_000_000
        ),
        name="layer",
    )(
        queries, latent_cache, value_up, out_proj.T, wgu, w_down[0], new_latent, hidden_in, norm_gain.reshape(1, -1),
        router.T, expert_ids.T, cache_lengths,
    )


def solution(mesh):
    in_specs = (
        P("batch", None),
        P("batch", ("sec", "head"), None),
        P("batch", None, None),
        P("batch", None),
        P("batch"),
        P(("sec", "head"), None, None),
        P(("sec", "head"), "batch"),
        P(),
        P(),
        P("batch", None),
        P("batch", None, None, ("sec", "head")),
        P("batch", ("sec", "head"), None),
    )
    out_specs = P("batch", ("sec", "head"))
    return jax.shard_map(body, mesh=mesh, in_specs=in_specs, out_specs=out_specs, check_vma=False)
```

```python
import jax
import jax.numpy as jnp
from jax import lax
from jax.experimental import pallas as pl
from jax.experimental.pallas import tpu as pltpu
from jax.sharding import PartitionSpec as P

QKD = 192
TOP = 8
norm_epsilon = 1e-06
route_scale = 2.5

BF16, F32 = jnp.bfloat16, jnp.float32
MESH = pl.DeviceIdType.MESH
PARTS = ((0, 768, 1408), (1408, 1920, 2304), (2304, 3072, 3712))
HALF = 3584
GROUP = 8


def dot(a, b):
    return lax.dot_general(a, b, (((1,), (0,)), ((), ())), preferred_element_type=F32)


def dot_t(a, b):
    return lax.dot_general(a, b, (((1,), (1,)), ((), ())), preferred_element_type=F32)


def layer_kernel(
    q_hbm, cache_hbm, vu_hbm, wo_hbm, wgu_hbm, wd_hbm, new_ref, hidden_ref, gain_ref, router_ref, ids_ref, len_ref,
    out_ref,
    CA, Q, NEW, L, VU, RAW, PERM, HID, GAIN, ROUT, HIT,
    H, WO, ACC, PS, RX, SS, RY, MS, MR, RF, RL, X, WGU, GU, WD, A, Y0, Y1, R0, R1, T0, T1, Q0, Q1, O0,
    ring_s, ring_r, bx_s, bx_r, by_s, by_r, m_s, m_r, rl_s, rl_r, wo_s, wo_r, wg_s, wg_r, wd_s, wd_r, wf_s, wf_r,
    y0_s, y0_r, y1_s, y1_r, y2_s, y2_r, loc, ca_sem, raw_sem,
):
    sec = lax.axis_index("sec")
    head = lax.axis_index("head")
    batch = lax.axis_index("batch")
    core = batch % 2
    y = (batch // 2) % 4
    z = batch // 8
    x = head * 2 + sec
    p = z * 4 + y

    def at(zz=None, yy=None, cc=None, xx=None):
        zz = z if zz is None else zz
        yy = y if yy is None else yy
        cc = core if cc is None else cc
        xx = x if xx is None else xx
        return (xx % 2, zz * 8 + yy * 2 + cc, xx // 2)

    barrier = pltpu.get_barrier_semaphore()

    def greet(to):
        pl.semaphore_signal(barrier, inc=1, device_id=to, device_id_type=MESH)

    greet(at(cc=1 - core))
    for d in range(1, 4):
        greet(at(xx=(x + d) % 4))
    for d in range(1, 16):
        q = (p + d) % 16
        greet(at(zz=q // 4, yy=q % 4))

    def rcopy(src, dst, send, recv, to):
        return pltpu.make_async_remote_copy(
            src_ref=src, dst_ref=dst, send_sem=send, recv_sem=recv, device_id=to, device_id_type=MESH
        )

    def lcopy(src, dst, k):
        return pltpu.make_async_copy(src, dst, loc.at[k])

    sends = []

    def go(copy):
        copy.start()
        sends.append(copy)
        return copy

    def cache_copy(g, slot):
        return pltpu.make_async_copy(
            cache_hbm.at[pl.ds(g * GROUP, GROUP)], CA.at[slot, :, pl.ds(0, 192)], ca_sem.at[slot]
        )

    def raw_copy(i, slot):
        rows = pl.ds(pl.multiple_of(i * 3584, 128), 3584)
        return pltpu.make_async_copy(wgu_hbm.at[rows], RAW.at[slot], raw_sem.at[slot])

    own_q = lcopy(q_hbm, Q, 0)
    own_q.start()
    cache_copy(0, 0).start()
    cache_copy(1, 1).start()
    own_vu = lcopy(vu_hbm, VU, 2)
    own_vu.start()
    own_wo = lcopy(wo_hbm, WO.at[core], 1)
    own_wo.start()

    def wd_cols(xx):
        s = (xx % 2) * 2 + xx // 2
        return wd_hbm.at[:, pl.ds(pl.multiple_of(s * 1792, 128), 1792)]

    NEW[...] = new_ref[...].astype(F32)
    own_q.wait()
    pl.semaphore_wait(barrier, 19)

    other_core = at(cc=1 - core)
    send_wo = go(rcopy(wo_hbm, WO.at[core], wo_s.at[0], wo_r.at[0], other_core))
    send_wd = []
    for d in (1, 3):
        xx = (x + d) % 4
        send_wd.append(go(rcopy(wd_cols(xx), WD.at[x, core], wd_s.at[d - 1], wd_r.at[d - 1], at(xx=xx))))
    opposite = (x + 2) % 4

    def far_wd(k, rows):
        src, dst = wd_cols(opposite).at[rows], WD.at[x, core, rows]
        send_wd.append(go(rcopy(src, dst, wd_s.at[k], wd_r.at[k], at(xx=opposite))))

    far_wd(1, pl.ds(0, 128))

    own_row = lax.broadcasted_iota(jnp.int32, (16, 576), 0) == 0
    column = lax.broadcasted_iota(jnp.int32, (GROUP * 32, 208), 1)

    def attend(g, carry):
        slot = g % 2
        cache_copy(g, slot).wait()
        news = [NEW[pl.ds(g * GROUP + i, 1), :] for i in range(GROUP)]
        for i in range(GROUP):
            CA[slot, i, 192:208, :] = jnp.where(own_row, news[i], 0.0).astype(BF16)
        lengths = jnp.concatenate([jnp.full((32, 1), len_ref[g * GROUP + i], jnp.int32) for i in range(GROUP)], axis=0)
        scores = jnp.concatenate([dot_t(Q[g * GROUP + i], CA[slot, i]) for i in range(GROUP)], axis=0) * (QKD**-0.5)
        scores = jnp.where((column < lengths) | (column == 192), scores, -jnp.inf)
        weights = jnp.exp(scores - jnp.max(scores, axis=1, keepdims=True))
        weights = (weights / jnp.sum(weights, axis=1, keepdims=True)).astype(BF16)
        for i in range(GROUP):
            rows = pl.ds(pl.multiple_of((g * GROUP + i) * 32, 32), 32)
            latent = dot(weights[i * 32 : i * 32 + 32], CA[slot, i, :, 0:512])
            for c in range(4):
                L[c, rows, :] = latent[:, c * 128 : c * 128 + 128]

        @pl.when(g + 2 < 32 // GROUP)
        def _():
            cache_copy(g + 2, slot).start()

        return carry

    lax.fori_loop(0, 32 // GROUP, attend, 0)
    raw_copy(0, 0).start()
    raw_copy(1, 1).start()
    own_wd = lcopy(wd_cols(x), WD.at[x, core], 3)
    own_wd.start()
    own_vu.wait()

    def head_values(i, carry):
        for j in range(4):
            h = i * 4 + j
            latent = jnp.concatenate([L[c, pl.ds(h, 32, stride=32), :] for c in range(4)], axis=1).astype(BF16)
            H[z, y, :, pl.ds(pl.multiple_of(h * 128, 128), 128)] = dot(latent, VU[h]).astype(BF16)
        return carry

    dims = {"z": z, "y": y, "x": x}

    def neighbour(dim, d):
        i = (dims[dim] + d) % 4
        return at(zz=i) if dim == "z" else at(yy=i) if dim == "y" else at(xx=i)

    class Ring:
        def __init__(self, k, dim, full, low, high):
            self.k, self.dim, self.full, self.low, self.high = k, dim, full, low, high

        def copy(self, part, i, d, j):
            i = (dims[self.dim] + i) % 4
            return rcopy(part(i), part(i), ring_s.at[self.k, j], ring_r.at[self.k, j], neighbour(self.dim, d))

        def start(self):
            self.up = go(self.copy(self.full, 0, 1, 0))
            self.down = go(self.copy(self.full, 0, 3, 1))

        def forward(self):
            self.up.wait_recv()
            self.far_up = go(self.copy(self.low, 3, 1, 2))
            self.down.wait_recv()
            self.far_down = go(self.copy(self.high, 1, 3, 3))

        def finish(self):
            self.far_up.wait_recv()
            self.far_down.wait_recv()

    def head_ring(k, dim, half, other):
        def view(rows):
            def part(i):
                cols = pl.ds(half * 2048, 2048)
                if dim == "z":
                    return H.at[i, (y + other) % 4, rows, cols]
                return H.at[(z + other) % 4, i, rows, cols]

            return part

        return Ring(k, dim, view(pl.ds(0, 32)), view(pl.ds(0, 16)), view(pl.ds(16, 16)))

    h0a, h0b = head_ring(0, "y", 0, 0), [head_ring(1 + o, "z", 0, o) for o in range(4)]
    h1a, h1b = head_ring(5, "z", 1, 0), [head_ring(6 + o, "y", 1, o) for o in range(4)]

    lax.fori_loop(0, 4, head_values, 0)
    h0a.start()
    h0b[0].start()
    lax.fori_loop(4, 8, head_values, 0)
    h1a.start()
    h1b[0].start()

    spread_row = lax.broadcasted_iota(jnp.int32, (256, 256), 0)
    spread_col = lax.broadcasted_iota(jnp.int32, (256, 256), 1)
    PERM[...] = jnp.where(spread_col == (spread_row % 64) * 4 + spread_row // 64, 1.0, 0.0).astype(BF16)

    def separate(i, carry):
        slot = i % 2
        raw_copy(i, slot).wait()
        for b in range(0, 14, 2):
            pair = jnp.concatenate([RAW[slot, b * 256 : b * 256 + 256], RAW[slot, b * 256 + 256 : b * 256 + 512]], axis=1)
            moved = dot(PERM[...], pair).astype(BF16)
            for j in range(2):
                for u in range(2):
                    k = (b + j) * 64 + u * 32
                    h, row = (k // 224) % 2, k // 448 * 224 + k % 224
                    row = pl.multiple_of(i * 448 + row, 32)
                    for q in range(4):
                        to = q % 2 * 256 + q // 2 * 128
                        a = q * 64 + u * 32
                        WGU[core, h, pl.ds(row, 32), to : to + 128] = moved[a : a + 32, j * 128 : j * 128 + 128]

        @pl.when(i + 2 < 8)
        def _():
            raw_copy(i + 2, slot).start()

        return carry

    def far_wgu(i, h):
        block = WGU.at[core, h, pl.ds(i * 448, 448)]
        return rcopy(block, block, wg_s.at[0], wg_r.at[0], other_core)

    wgu_all = rcopy(WGU.at[core], WGU.at[core], wg_s.at[0], wg_r.at[0], other_core)

    def pieces(v):
        return [jnp.where(sec == 0, v[:, i * 448 : i * 448 + 224], v[:, i * 448 + 224 : i * 448 + 448]) for i in range(16)]

    def pack_inputs():
        for i, piece in enumerate(pieces(hidden_ref[pl.ds(pl.multiple_of(head * 16, 16), 16), :].astype(F32))):
            HID[i] = piece
        GAIN[...] = jnp.concatenate(pieces(gain_ref[...]), axis=1)
        ROUT[0:32, :] = jnp.concatenate(pieces(router_ref[...].astype(F32)), axis=1).astype(BF16)
        ROUT[32:128, :] = jnp.zeros((96, HALF), BF16)
        expert = lax.broadcasted_iota(jnp.int32, (128, 32), 0)
        hit = jnp.zeros((128, 32), F32)
        for k in range(TOP):
            hit += jnp.where(ids_ref[k : k + 1, :] == expert, 1.0, 0.0)
        mine = lax.broadcasted_iota(jnp.int32, (16, 32), 1) == lax.broadcasted_iota(jnp.int32, (16, 32), 0) + head * 16
        HIT[...] = dot_t(jnp.where(mine, 1.0, 0.0).astype(BF16), hit.astype(BF16))

    ACC[...] = jnp.zeros_like(ACC)
    lax.fori_loop(0, 1, separate, 0)
    h0a.forward()
    h1a.forward()
    for o in (1, 3):
        h0b[o].start()
        h1b[o].start()
    lax.fori_loop(1, 2, separate, 0)
    h0b[0].forward()
    h1b[0].forward()
    h0a.finish()
    h0b[2].start()
    h1a.finish()
    h1b[2].start()
    lax.fori_loop(2, 4, separate, 0)
    for i in range(4):
        for h in range(2):
            far_wgu(i, h).start()
    lax.fori_loop(4, 7, separate, 0)
    for o in (1, 3):
        h0b[o].forward()
        h1b[o].forward()
    lax.fori_loop(7, 8, separate, 0)
    pack_inputs()
    for i in range(4, 8):
        for h in range(2):
            far_wgu(i, h).start()

    own_wo.wait()
    send_wo.wait_recv()

    def project_z(zz):
        rows = H[zz, :, :, 0:2048].reshape(128, 2048)
        for n in range(2):
            ACC[n, zz] += dot_t(rows, WO[n, :, 0:2048]).reshape(4, 32, 224)

    def project_y(yy):
        rows = H[:, yy, :, 2048:4096].reshape(128, 2048)
        for n in range(2):
            ACC[n, :, yy] += dot_t(rows, WO[n, :, 2048:4096]).reshape(4, 32, 224)

    def project(d):
        project_z((z + d) % 4)
        project_y((y + d) % 4)

    project(0)
    h0b[2].forward()
    h1b[2].forward()
    project(1)
    project(3)
    for o in range(4):
        h0b[o].finish()
        h1b[o].finish()
    project(2)

    for r in range(2):
        for h in range(2):
            PS[r * 2 + h] = ACC[h, :, :, r * 16 : r * 16 + 16, :].astype(BF16)
    cross = []
    for d in (2, 1, 3):
        xx = (x + d) % 4
        cross.append(go(rcopy(PS.at[xx], RX.at[x], bx_s.at[d - 1], bx_r.at[d - 1], at(xx=xx))))
    far_wd(3, pl.ds(128, 128))
    for c in cross:
        c.wait_recv()
    total = PS[x].astype(F32)
    for d in range(1, 4):
        total += RX[(x + d) % 4].astype(F32)
    SS[...] = total.astype(BF16)
    plane = []
    for d in range(1, 16):
        q = (p + d) % 16
        plane.append(go(rcopy(SS.at[q // 4, q % 4], RY.at[p], by_s.at[d - 1], by_r.at[d - 1], at(zz=q // 4, yy=q % 4))))
    RY[p] = SS[z, y]
    for c in plane:
        c.wait_recv()

    RF[...] = RY[...].astype(F32) + HID[...]
    res = jnp.concatenate([RF[i] for i in range(16)], axis=1)
    scaled = res * GAIN[...]
    lane = lax.broadcasted_iota(jnp.int32, (16, 128), 1)
    square = jnp.sum(res * res, axis=1, keepdims=True)
    note = dot_t(scaled.astype(BF16), ROUT[...])
    MS[...] = jnp.where(lane == 32, square, note)
    X[z, y, head, sec, :, 0:HALF] = scaled.astype(BF16)
    msg = go(rcopy(MS, MR, m_s.at[0], m_r.at[0], at(xx=x + 1 - 2 * sec)))
    def row_ring(k, part, dim, done, fixed):
        c0, c1, c2 = PARTS[part]

        def view(a, b):
            def block(i):
                at_dim = {}
                for d in "zyx":
                    at_dim[d] = i if d == dim else None if d in done else (dims[d] + fixed.get(d, 0)) % 4
                zi, yi, xi = (slice(None) if at_dim[d] is None else at_dim[d] for d in "zyx")
                if at_dim["x"] is None:
                    return X.at[zi, yi, :, :, :, pl.ds(a, b - a)]
                return X.at[zi, yi, xi // 2, xi % 2, :, pl.ds(a, b - a)]

            return block

        return Ring(k, dim, view(c0, c2), view(c0, c1), view(c1, c2))

    first, second, third = [], [], []
    for part, (d1, d2, d3) in enumerate(("xyz", "yzx", "zxy")):
        first.append(row_ring(10 + part, part, d1, "", {}))
        second.append(row_ring(13 + part, part, d2, d1, {}))
        third.append([row_ring(16 + part * 4 + o, part, d3, d1, {d2: o}) for o in range(4)])
    GU[...] = jnp.zeros_like(GU)
    first[0].start()
    first[1].start()

    msg.wait_recv()
    both = MS[...] + MR[...]
    mean_square = jnp.sum(jnp.where(lane == 32, both, 0.0), axis=1, keepdims=True) / (2 * HALF)
    inv = lax.rsqrt(mean_square + norm_epsilon)
    affinity = jax.nn.sigmoid(both * inv)
    picked = jnp.where(HIT[...] > 0.0, affinity, 0.0)
    gate = route_scale * picked / jnp.sum(picked, axis=1, keepdims=True)
    gate = jnp.where(lane == 32, inv, gate)
    top = gate.astype(BF16).astype(F32)
    X[z, y, head, sec, :, HALF:] = (top + pltpu.roll(gate - top, 64, 1)).astype(BF16)
    first[2].start()

    for ring in first:
        ring.forward()
    for before, ring in zip(first, second):
        before.finish()
        ring.start()
    for rings in third:
        rings[0].start()
    for ring in second:
        ring.forward()
    for rings in third:
        rings[1].start()
        rings[3].start()

    to_out = []
    for d in range(1, 4):
        xx = (x + d) % 4
        s = (xx % 2) * 2 + xx // 2
        to_out.append(go(rcopy(RF.at[pl.ds(s * 4, 4)], RL.at[x], rl_s.at[d - 1], rl_r.at[d - 1], at(xx=xx))))
    RL[x] = RF[pl.ds((sec * 2 + head) * 4, 4)]
    for rings in third:
        rings[0].forward()
    for before, rings in zip(second, third):
        before.finish()
        rings[2].start()

    for c in send_wd:
        c.wait_recv()
    own_wd.wait()

    pass_on = []
    for i in range(4):
        pass_on.append(go(rcopy(WD.at[i, core], WD.at[i, core], wf_s.at[i], wf_r.at[i], other_core)))
    wgu_all.wait_recv()

    def cols(part):
        return PARTS[part][0], min(PARTS[part][2], HALF)

    def experts_z(zz):
        a, b = cols(0)
        for h in range(2):
            rows = X[zz, :, :, h, :, a:b].reshape(128, b - a)
            for e in range(2):
                GU[e, zz] += dot(rows, WGU[e, h, a:b]).reshape(4, 2, 16, 512)

    def experts_x(xx):
        a, b = cols(1)
        r, h = xx // 2, xx % 2
        rows = X[:, :, r, h, :, a:b].reshape(256, b - a)
        for e in range(2):
            GU[e, :, :, r] += dot(rows, WGU[e, h, a:b]).reshape(4, 4, 16, 512)

    def experts_y(yy):
        a, b = cols(2)
        for h in range(2):
            rows = X[:, yy, :, h, :, a:b].reshape(128, b - a)
            for e in range(2):
                GU[e, :, yy] += dot(rows, WGU[e, h, a:b]).reshape(4, 2, 16, 512)

    def experts(d):
        experts_z((z + d) % 4)
        experts_x((x + d) % 4)
        experts_y((y + d) % 4)

    experts(0)
    for o in (1, 3, 2):
        for rings in third:
            rings[o].forward()
    experts(1)
    experts(3)
    for o in range(4):
        for rings in third:
            rings[o].finish()
    experts(2)

    wide = lax.broadcasted_iota(jnp.int32, (128, 128), 1) % 64

    def activate(zz):
        gates = X[zz, :, :, 0, :, HALF:].reshape(128, 128).astype(F32)
        inv = jnp.sum(jnp.where(wide == 32, gates, 0.0), axis=1, keepdims=True)
        for e in range(2):
            weight = jnp.sum(jnp.where(wide == p * 2 + e, gates, 0.0), axis=1, keepdims=True)
            gu = GU[e, zz].reshape(128, 512) * inv
            act = jax.nn.silu(gu[:, :256]) * gu[:, 256:] * weight
            A[x, zz, :, :, e * 256 : e * 256 + 256] = act.astype(BF16).reshape(4, 32, 256)

    def act_ring(j):
        zz = (z + order[j]) % 4
        return Ring(
            28 + j, "x", lambda i: A.at[i, zz], lambda i: A.at[i, zz, pl.ds(0, 2)], lambda i: A.at[i, zz, pl.ds(2, 2)]
        )

    order = (2, 1, 3, 0)
    acts = [act_ring(j) for j in range(4)]
    over_y, over_z, last_z, last_y = [], [], [], []

    def down(j):
        zz = (z + order[j]) % 4
        for half, buf in ((1, Y1), (0, Y0)):
            acc = jnp.zeros((128, 896), F32)
            for i in range(4):
                acc += dot(A[i, zz].reshape(128, 512), WD[i, :, :, half * 896 : half * 896 + 896].reshape(512, 896))
            buf[j] = acc.reshape(4, 32, 896).astype(BF16)
            if half == 1 and j < 3:
                over_z.append(go(rcopy(Y1.at[j], R1.at[j], y1_s.at[j], y1_r.at[j], at(zz=zz))))
        group = []
        for m in range(3):
            yy = (y + order[m]) % 4
            group.append(go(rcopy(Y0.at[j, yy], R0.at[j, m], y0_s.at[j, m], y0_r.at[j, m], at(yy=yy))))
        over_y.append(group)

    def gather_y(j):
        zz = (z + order[j]) % 4
        for c in over_y[j]:
            c.wait_recv()
        acc = Y0[j, y].astype(F32)
        for m in range(3):
            acc += R0[j, m].astype(F32)
        if j < 3:
            T0[j] = acc.astype(BF16)
            last_z.append(go(rcopy(T0.at[j], Q0.at[j], y2_s.at[0, j], y2_r.at[0, j], at(zz=zz))))
        else:
            O0[...] = acc

    activate((z + order[0]) % 4)
    acts[0].start()
    activate((z + order[1]) % 4)
    acts[1].start()
    activate((z + order[2]) % 4)
    activate((z + order[3]) % 4)
    acts[0].forward()
    acts[2].start()
    for c in pass_on:
        c.wait_recv()
    acts[1].forward()
    acts[0].finish()
    acts[3].start()
    down(0)
    acts[2].forward()
    acts[1].finish()
    down(1)
    gather_y(0)
    acts[3].forward()
    acts[2].finish()
    down(2)
    gather_y(1)
    acts[3].finish()
    down(3)
    gather_y(2)
    for c in over_z:
        c.wait_recv()

    def sum_z(yy):
        acc = Y1[3, yy].astype(F32)
        for m in range(3):
            acc += R1[m, yy].astype(F32)
        return acc

    for m in range(3):
        yy = (y + order[m]) % 4
        T1[m] = sum_z(yy).astype(BF16)
        last_y.append(go(rcopy(T1.at[m], Q1.at[m], y2_s.at[1, m], y2_r.at[1, m], at(yy=yy))))
    gather_y(3)
    m0 = O0[...]
    m1 = sum_z(y)
    for c in to_out + last_z + last_y:
        c.wait_recv()
    for m in range(3):
        m0 += Q0[m].astype(F32)
        m1 += Q1[m].astype(F32)
    for r in range(2):
        rows = slice(r * 16, r * 16 + 16)
        low = jnp.concatenate([RL[r * 2 + h, i] for i in range(2) for h in range(2)], axis=1)
        high = jnp.concatenate([RL[r * 2 + h, i] for i in range(2, 4) for h in range(2)], axis=1)
        out_ref[rows, 0:896] = (low + m0[rows]).astype(BF16)
        out_ref[rows, 896:1792] = (high + m1[rows]).astype(BF16)

    for c in sends:
        c.wait_send()
    wgu_all.wait_send()


def body(
    hidden_in, queries, latent_cache, new_latent, cache_lengths, value_up, out_proj, norm_gain, router, expert_ids,
    w_gate_up, w_down,
):
    wgu = w_gate_up[0].reshape(7168, 2, 2, 128).transpose(0, 2, 1, 3).reshape(28672, 128)
    any_spec = pl.BlockSpec(memory_space=pl.ANY)
    vmem = pl.BlockSpec(memory_space=pltpu.VMEM)
    dma = pltpu.SemaphoreType.DMA
    return pl.pallas_call(
        layer_kernel,
        out_shape=jax.ShapeDtypeStruct((32, 1792), BF16),
        in_specs=[any_spec] * 6 + [vmem] * 5 + [pl.BlockSpec(memory_space=pltpu.SMEM)],
        out_specs=vmem,
        scratch_shapes=[
            pltpu.VMEM((2, GROUP, 208, 576), BF16),
            pltpu.VMEM((32, 32, 576), BF16),
            pltpu.VMEM((32, 576), F32),
            pltpu.VMEM((4, 1024, 128), F32),
            pltpu.VMEM((32, 512, 128), BF16),
            pltpu.VMEM((2, 3584, 128), BF16),
            pltpu.VMEM((256, 256), BF16),
            pltpu.VMEM((16, 16, 224), F32),
            pltpu.VMEM((1, HALF), F32),
            pltpu.VMEM((128, HALF), BF16),
            pltpu.VMEM((16, 128), F32),
            pltpu.VMEM((4, 4, 32, 4096), BF16),
            pltpu.VMEM((2, 224, 4096), BF16),
            pltpu.VMEM((2, 4, 4, 32, 224), F32),
            pltpu.VMEM((4, 4, 4, 16, 224), BF16),
            pltpu.VMEM((4, 4, 4, 16, 224), BF16),
            pltpu.VMEM((4, 4, 16, 224), BF16),
            pltpu.VMEM((16, 16, 224), BF16),
            pltpu.VMEM((16, 128), F32),
            pltpu.VMEM((16, 128), F32),
            pltpu.VMEM((16, 16, 224), F32),
            pltpu.VMEM((4, 4, 16, 224), F32),
            pltpu.VMEM((4, 4, 2, 2, 16, 3712), BF16),
            pltpu.VMEM((2, 2, HALF, 512), BF16),
            pltpu.VMEM((2, 4, 4, 2, 16, 512), F32),
            pltpu.VMEM((4, 2, 256, 1792), BF16),
            pltpu.VMEM((4, 4, 4, 32, 512), BF16),
            pltpu.VMEM((4, 4, 32, 896), BF16),
            pltpu.VMEM((4, 4, 32, 896), BF16),
            pltpu.VMEM((4, 3, 32, 896), BF16),
            pltpu.VMEM((3, 4, 32, 896), BF16),
            pltpu.VMEM((3, 32, 896), BF16),
            pltpu.VMEM((3, 32, 896), BF16),
            pltpu.VMEM((3, 32, 896), BF16),
            pltpu.VMEM((3, 32, 896), BF16),
            pltpu.VMEM((32, 896), F32),
            dma((32, 4)),
            dma((32, 4)),
            dma((3,)),
            dma((3,)),
            dma((15,)),
            dma((15,)),
            dma((1,)),
            dma((1,)),
            dma((3,)),
            dma((3,)),
            dma((1,)),
            dma((1,)),
            dma((1,)),
            dma((1,)),
            dma((4,)),
            dma((4,)),
            dma((4,)),
            dma((4,)),
            dma((4, 3)),
            dma((4, 3)),
            dma((3,)),
            dma((3,)),
            dma((2, 3)),
            dma((2, 3)),
            dma((4,)),
            dma((2,)),
            dma((2,)),
        ],
        compiler_params=pltpu.CompilerParams(
            collective_id=0, has_side_effects=True, vmem_limit_bytes=66_000_000
        ),
        name="layer",
    )(
        queries, latent_cache, value_up, out_proj.T, wgu, w_down[0], new_latent, hidden_in, norm_gain.reshape(1, -1),
        router.T, expert_ids.T, cache_lengths,
    )


def solution(mesh):
    in_specs = (
        P("batch", None),
        P("batch", ("sec", "head"), None),
        P("batch", None, None),
        P("batch", None),
        P("batch"),
        P(("sec", "head"), None, None),
        P(("sec", "head"), "batch"),
        P(),
        P(),
        P("batch", None),
        P("batch", None, None, ("sec", "head")),
        P("batch", ("sec", "head"), None),
    )
    out_specs = P("batch", ("sec", "head"))
    return jax.shard_map(body, mesh=mesh, in_specs=in_specs, out_specs=out_specs, check_vma=False)
```

```python
import jax
import jax.numpy as jnp
from jax import lax
from jax.experimental import pallas as pl
from jax.experimental.pallas import tpu as pltpu
from jax.sharding import PartitionSpec as P

QKD = 192
TOP = 8
norm_epsilon = 1e-06
route_scale = 2.5

BF16, F32 = jnp.bfloat16, jnp.float32
MESH = pl.DeviceIdType.MESH
PARTS = ((0, 768, 1408), (1408, 1920, 2304), (2304, 3072, 3712))
HALF = 3584
GROUP = 8


def dot(a, b):
    return lax.dot_general(a, b, (((1,), (0,)), ((), ())), preferred_element_type=F32)


def dot_t(a, b):
    return lax.dot_general(a, b, (((1,), (1,)), ((), ())), preferred_element_type=F32)


def layer_kernel(
    q_hbm, cache_hbm, vu_hbm, wo_hbm, wgu_hbm, wd_hbm, new_ref, hidden_ref, gain_ref, router_ref, ids_ref, len_ref,
    out_ref,
    CA, Q, NEW, L, VU, RAW, PERM, HID, GAIN, ROUT, HIT,
    H, WO, ACC, PS, RX, MS, MR, RF, RL, X, WGU, GU, WD, A, Y0, Y1, R0, R1, T0, T1, Q0, Q1, O0,
    ring_s, ring_r, by_s, by_r, m_s, m_r, rl_s, rl_r, wo_s, wo_r, wg_s, wg_r, wd_s, wd_r, wf_s, wf_r,
    y0_s, y0_r, y1_s, y1_r, y2_s, y2_r, loc, ca_sem, raw_sem,
):
    sec = lax.axis_index("sec")
    head = lax.axis_index("head")
    batch = lax.axis_index("batch")
    core = batch % 2
    y = (batch // 2) % 4
    z = batch // 8
    x = head * 2 + sec
    p = z * 4 + y

    def at(zz=None, yy=None, cc=None, xx=None):
        zz = z if zz is None else zz
        yy = y if yy is None else yy
        cc = core if cc is None else cc
        xx = x if xx is None else xx
        return (xx % 2, zz * 8 + yy * 2 + cc, xx // 2)

    barrier = pltpu.get_barrier_semaphore()

    def greet(to):
        pl.semaphore_signal(barrier, inc=1, device_id=to, device_id_type=MESH)

    greet(at(cc=1 - core))

    def offset(i):
        return (z + i // 16) % 4, (y + i // 4 % 4) % 4, (x + i % 4) % 4

    def greet_step(i, carry):
        zz, yy, xx = offset(i)
        greet(at(zz=zz, yy=yy, xx=xx))
        return carry

    lax.fori_loop(1, 64, greet_step, 0)

    def rcopy(src, dst, send, recv, to):
        return pltpu.make_async_remote_copy(
            src_ref=src, dst_ref=dst, send_sem=send, recv_sem=recv, device_id=to, device_id_type=MESH
        )

    def lcopy(src, dst, k):
        return pltpu.make_async_copy(src, dst, loc.at[k])

    sends = []

    def go(copy):
        copy.start()
        sends.append(copy)
        return copy

    def cache_copy(g, slot):
        return pltpu.make_async_copy(
            cache_hbm.at[pl.ds(g * GROUP, GROUP)], CA.at[slot, :, pl.ds(0, 192)], ca_sem.at[slot]
        )

    def raw_copy(i, slot):
        rows = pl.ds(pl.multiple_of(i * 3584, 128), 3584)
        return pltpu.make_async_copy(wgu_hbm.at[rows], RAW.at[slot], raw_sem.at[slot])

    own_q = lcopy(q_hbm, Q, 0)
    own_q.start()
    cache_copy(0, 0).start()
    cache_copy(1, 1).start()
    own_vu = lcopy(vu_hbm, VU, 2)
    own_vu.start()
    own_wo = lcopy(wo_hbm, WO.at[core], 1)
    own_wo.start()

    def wd_cols(xx):
        s = (xx % 2) * 2 + xx // 2
        return wd_hbm.at[:, pl.ds(pl.multiple_of(s * 1792, 128), 1792)]

    NEW[...] = new_ref[...].astype(F32)
    own_q.wait()
    pl.semaphore_wait(barrier, 64)

    other_core = at(cc=1 - core)
    send_wo = go(rcopy(wo_hbm, WO.at[core], wo_s.at[0], wo_r.at[0], other_core))
    send_wd = []
    for d in (1, 3):
        xx = (x + d) % 4
        send_wd.append(go(rcopy(wd_cols(xx), WD.at[x, core], wd_s.at[d - 1], wd_r.at[d - 1], at(xx=xx))))
    opposite = (x + 2) % 4

    def far_wd(k, rows):
        src, dst = wd_cols(opposite).at[rows], WD.at[x, core, rows]
        send_wd.append(go(rcopy(src, dst, wd_s.at[k], wd_r.at[k], at(xx=opposite))))

    far_wd(1, pl.ds(0, 128))

    own_row = lax.broadcasted_iota(jnp.int32, (16, 576), 0) == 0
    column = lax.broadcasted_iota(jnp.int32, (GROUP * 32, 208), 1)

    def attend(g, carry):
        slot = g % 2
        cache_copy(g, slot).wait()
        news = [NEW[pl.ds(g * GROUP + i, 1), :] for i in range(GROUP)]
        for i in range(GROUP):
            CA[slot, i, 192:208, :] = jnp.where(own_row, news[i], 0.0).astype(BF16)
        lengths = jnp.concatenate([jnp.full((32, 1), len_ref[g * GROUP + i], jnp.int32) for i in range(GROUP)], axis=0)
        scores = jnp.concatenate([dot_t(Q[g * GROUP + i], CA[slot, i]) for i in range(GROUP)], axis=0) * (QKD**-0.5)
        scores = jnp.where((column < lengths) | (column == 192), scores, -jnp.inf)
        weights = jnp.exp(scores - jnp.max(scores, axis=1, keepdims=True))
        weights = (weights / jnp.sum(weights, axis=1, keepdims=True)).astype(BF16)
        for i in range(GROUP):
            rows = pl.ds(pl.multiple_of((g * GROUP + i) * 32, 32), 32)
            latent = dot(weights[i * 32 : i * 32 + 32], CA[slot, i, :, 0:512])
            for c in range(4):
                L[c, rows, :] = latent[:, c * 128 : c * 128 + 128]

        @pl.when(g + 2 < 32 // GROUP)
        def _():
            cache_copy(g + 2, slot).start()

        return carry

    lax.fori_loop(0, 32 // GROUP, attend, 0)
    raw_copy(0, 0).start()
    raw_copy(1, 1).start()
    own_wd = lcopy(wd_cols(x), WD.at[x, core], 3)
    own_wd.start()
    own_vu.wait()

    def head_values(i, carry):
        for j in range(4):
            h = i * 4 + j
            latent = jnp.concatenate([L[c, pl.ds(h, 32, stride=32), :] for c in range(4)], axis=1).astype(BF16)
            H[z, y, :, pl.ds(pl.multiple_of(h * 128, 128), 128)] = dot(latent, VU[h]).astype(BF16)
        return carry

    dims = {"z": z, "y": y, "x": x}

    def neighbour(dim, d):
        i = (dims[dim] + d) % 4
        return at(zz=i) if dim == "z" else at(yy=i) if dim == "y" else at(xx=i)

    class Ring:
        def __init__(self, k, dim, full, low, high):
            self.k, self.dim, self.full, self.low, self.high = k, dim, full, low, high

        def copy(self, part, i, d, j):
            i = (dims[self.dim] + i) % 4
            return rcopy(part(i), part(i), ring_s.at[self.k, j], ring_r.at[self.k, j], neighbour(self.dim, d))

        def start(self):
            self.up = go(self.copy(self.full, 0, 1, 0))
            self.down = go(self.copy(self.full, 0, 3, 1))

        def forward(self):
            self.up.wait_recv()
            self.far_up = go(self.copy(self.low, 3, 1, 2))
            self.down.wait_recv()
            self.far_down = go(self.copy(self.high, 1, 3, 3))

        def finish(self):
            self.far_up.wait_recv()
            self.far_down.wait_recv()

    def head_ring(k, dim, half, other):
        def view(rows):
            def part(i):
                cols = pl.ds(half * 2048, 2048)
                if dim == "z":
                    return H.at[i, (y + other) % 4, rows, cols]
                return H.at[(z + other) % 4, i, rows, cols]

            return part

        return Ring(k, dim, view(pl.ds(0, 32)), view(pl.ds(0, 16)), view(pl.ds(16, 16)))

    h0a, h0b = head_ring(0, "y", 0, 0), [head_ring(1 + o, "z", 0, o) for o in range(4)]
    h1a, h1b = head_ring(5, "z", 1, 0), [head_ring(6 + o, "y", 1, o) for o in range(4)]

    lax.fori_loop(0, 4, head_values, 0)
    h0a.start()
    h0b[0].start()
    lax.fori_loop(4, 8, head_values, 0)
    h1a.start()
    h1b[0].start()

    spread_row = lax.broadcasted_iota(jnp.int32, (256, 256), 0)
    spread_col = lax.broadcasted_iota(jnp.int32, (256, 256), 1)
    PERM[...] = jnp.where(spread_col == (spread_row % 64) * 4 + spread_row // 64, 1.0, 0.0).astype(BF16)

    def separate(i, carry):
        slot = i % 2
        raw_copy(i, slot).wait()
        for b in range(0, 14, 2):
            pair = jnp.concatenate([RAW[slot, b * 256 : b * 256 + 256], RAW[slot, b * 256 + 256 : b * 256 + 512]], axis=1)
            moved = dot(PERM[...], pair).astype(BF16)
            for j in range(2):
                for u in range(2):
                    k = (b + j) * 64 + u * 32
                    h, row = (k // 224) % 2, k // 448 * 224 + k % 224
                    row = pl.multiple_of(i * 448 + row, 32)
                    for q in range(4):
                        to = q % 2 * 256 + q // 2 * 128
                        a = q * 64 + u * 32
                        WGU[core, h, pl.ds(row, 32), to : to + 128] = moved[a : a + 32, j * 128 : j * 128 + 128]

        @pl.when(i + 2 < 8)
        def _():
            raw_copy(i + 2, slot).start()

        return carry

    def far_wgu(i, h):
        block = WGU.at[core, h, pl.ds(i * 448, 448)]
        return rcopy(block, block, wg_s.at[0], wg_r.at[0], other_core)

    wgu_all = rcopy(WGU.at[core], WGU.at[core], wg_s.at[0], wg_r.at[0], other_core)

    def pieces(v):
        return [jnp.where(sec == 0, v[:, i * 448 : i * 448 + 224], v[:, i * 448 + 224 : i * 448 + 448]) for i in range(16)]

    def pack_inputs():
        for i, piece in enumerate(pieces(hidden_ref[pl.ds(pl.multiple_of(head * 16, 16), 16), :].astype(F32))):
            HID[i] = piece
        GAIN[...] = jnp.concatenate(pieces(gain_ref[...]), axis=1)
        ROUT[0:32, :] = jnp.concatenate(pieces(router_ref[...].astype(F32)), axis=1).astype(BF16)
        ROUT[32:128, :] = jnp.zeros((96, HALF), BF16)
        expert = lax.broadcasted_iota(jnp.int32, (128, 32), 0)
        hit = jnp.zeros((128, 32), F32)
        for k in range(TOP):
            hit += jnp.where(ids_ref[k : k + 1, :] == expert, 1.0, 0.0)
        mine = lax.broadcasted_iota(jnp.int32, (16, 32), 1) == lax.broadcasted_iota(jnp.int32, (16, 32), 0) + head * 16
        HIT[...] = dot_t(jnp.where(mine, 1.0, 0.0).astype(BF16), hit.astype(BF16))

    ACC[...] = jnp.zeros_like(ACC)
    lax.fori_loop(0, 1, separate, 0)
    h0a.forward()
    h1a.forward()
    for o in (1, 3):
        h0b[o].start()
        h1b[o].start()
    lax.fori_loop(1, 2, separate, 0)
    h0b[0].forward()
    h1b[0].forward()
    h0a.finish()
    h0b[2].start()
    h1a.finish()
    h1b[2].start()
    lax.fori_loop(2, 4, separate, 0)
    for i in range(4):
        for h in range(2):
            far_wgu(i, h).start()
    lax.fori_loop(4, 7, separate, 0)
    for o in (1, 3):
        h0b[o].forward()
        h1b[o].forward()
    lax.fori_loop(7, 8, separate, 0)
    pack_inputs()
    for i in range(4, 8):
        for h in range(2):
            far_wgu(i, h).start()

    own_wo.wait()
    send_wo.wait_recv()

    def project_z(zz):
        rows = H[zz, :, :, 0:2048].reshape(128, 2048)
        for n in range(2):
            ACC[n, zz] += dot_t(rows, WO[n, :, 0:2048]).reshape(4, 32, 224)

    def project_y(yy):
        rows = H[:, yy, :, 2048:4096].reshape(128, 2048)
        for n in range(2):
            ACC[n, :, yy] += dot_t(rows, WO[n, :, 2048:4096]).reshape(4, 32, 224)

    def project(d):
        project_z((z + d) % 4)
        project_y((y + d) % 4)

    project(0)
    h0b[2].forward()
    h1b[2].forward()
    project(1)
    project(3)
    for o in range(4):
        h0b[o].finish()
        h1b[o].finish()
    project(2)

    for r in range(2):
        for h in range(2):
            PS[r * 2 + h] = ACC[h, :, :, r * 16 : r * 16 + 16, :].astype(BF16)

    def partial_copy(i):
        zz, yy, xx = offset(i)
        return rcopy(PS.at[xx, zz, yy], RX.at[x, p], by_s.at[i - 1], by_r.at[i - 1], at(zz=zz, yy=yy, xx=xx))

    def partial_start(i, carry):
        partial_copy(64 - i).start()
        return carry

    def partial_arrived(i, carry):
        partial_copy(64 - i).wait_recv()
        return carry

    def partial_sent(i, carry):
        partial_copy(i).wait_send()
        return carry

    lax.fori_loop(1, 64, partial_start, 0)
    far_wd(3, pl.ds(128, 128))
    RX[x, p] = PS[x, z, y]
    lax.fori_loop(1, 64, partial_arrived, 0)

    total = HID[...]
    for i in range(4):
        total += RX[i].astype(F32)
    RF[...] = total
    res = jnp.concatenate([RF[i] for i in range(16)], axis=1)
    scaled = res * GAIN[...]
    lane = lax.broadcasted_iota(jnp.int32, (16, 128), 1)
    square = jnp.sum(res * res, axis=1, keepdims=True)
    note = dot_t(scaled.astype(BF16), ROUT[...])
    MS[...] = jnp.where(lane == 32, square, note)
    X[z, y, head, sec, :, 0:HALF] = scaled.astype(BF16)
    msg = go(rcopy(MS, MR, m_s.at[0], m_r.at[0], at(xx=x + 1 - 2 * sec)))
    def row_ring(k, part, dim, done, fixed):
        c0, c1, c2 = PARTS[part]

        def view(a, b):
            def block(i):
                at_dim = {}
                for d in "zyx":
                    at_dim[d] = i if d == dim else None if d in done else (dims[d] + fixed.get(d, 0)) % 4
                zi, yi, xi = (slice(None) if at_dim[d] is None else at_dim[d] for d in "zyx")
                if at_dim["x"] is None:
                    return X.at[zi, yi, :, :, :, pl.ds(a, b - a)]
                return X.at[zi, yi, xi // 2, xi % 2, :, pl.ds(a, b - a)]

            return block

        return Ring(k, dim, view(c0, c2), view(c0, c1), view(c1, c2))

    first, second, third = [], [], []
    for part, (d1, d2, d3) in enumerate(("xyz", "yzx", "zxy")):
        first.append(row_ring(10 + part, part, d1, "", {}))
        second.append(row_ring(13 + part, part, d2, d1, {}))
        third.append([row_ring(16 + part * 4 + o, part, d3, d1, {d2: o}) for o in range(4)])
    GU[...] = jnp.zeros_like(GU)
    first[0].start()
    first[1].start()

    msg.wait_recv()
    both = MS[...] + MR[...]
    mean_square = jnp.sum(jnp.where(lane == 32, both, 0.0), axis=1, keepdims=True) / (2 * HALF)
    inv = lax.rsqrt(mean_square + norm_epsilon)
    affinity = jax.nn.sigmoid(both * inv)
    picked = jnp.where(HIT[...] > 0.0, affinity, 0.0)
    gate = route_scale * picked / jnp.sum(picked, axis=1, keepdims=True)
    gate = jnp.where(lane == 32, inv, gate)
    top = gate.astype(BF16).astype(F32)
    X[z, y, head, sec, :, HALF:] = (top + pltpu.roll(gate - top, 64, 1)).astype(BF16)
    first[2].start()

    for ring in first:
        ring.forward()
    for before, ring in zip(first, second):
        before.finish()
        ring.start()
    for rings in third:
        rings[0].start()
    for ring in second:
        ring.forward()
    for rings in third:
        rings[1].start()
        rings[3].start()

    to_out = []
    for d in range(1, 4):
        xx = (x + d) % 4
        s = (xx % 2) * 2 + xx // 2
        to_out.append(go(rcopy(RF.at[pl.ds(s * 4, 4)], RL.at[x], rl_s.at[d - 1], rl_r.at[d - 1], at(xx=xx))))
    RL[x] = RF[pl.ds((sec * 2 + head) * 4, 4)]
    for rings in third:
        rings[0].forward()
    for before, rings in zip(second, third):
        before.finish()
        rings[2].start()

    for c in send_wd:
        c.wait_recv()
    own_wd.wait()

    pass_on = []
    for i in range(4):
        pass_on.append(go(rcopy(WD.at[i, core], WD.at[i, core], wf_s.at[i], wf_r.at[i], other_core)))
    wgu_all.wait_recv()

    def cols(part):
        return PARTS[part][0], min(PARTS[part][2], HALF)

    def experts_z(zz):
        a, b = cols(0)
        for h in range(2):
            rows = X[zz, :, :, h, :, a:b].reshape(128, b - a)
            for e in range(2):
                GU[e, zz] += dot(rows, WGU[e, h, a:b]).reshape(4, 2, 16, 512)

    def experts_x(xx):
        a, b = cols(1)
        r, h = xx // 2, xx % 2
        rows = X[:, :, r, h, :, a:b].reshape(256, b - a)
        for e in range(2):
            GU[e, :, :, r] += dot(rows, WGU[e, h, a:b]).reshape(4, 4, 16, 512)

    def experts_y(yy):
        a, b = cols(2)
        for h in range(2):
            rows = X[:, yy, :, h, :, a:b].reshape(128, b - a)
            for e in range(2):
                GU[e, :, yy] += dot(rows, WGU[e, h, a:b]).reshape(4, 2, 16, 512)

    def experts(d):
        experts_z((z + d) % 4)
        experts_x((x + d) % 4)
        experts_y((y + d) % 4)

    experts(0)
    for o in (1, 3, 2):
        for rings in third:
            rings[o].forward()
    experts(1)
    experts(3)
    for o in range(4):
        for rings in third:
            rings[o].finish()
    experts(2)

    wide = lax.broadcasted_iota(jnp.int32, (128, 128), 1) % 64

    def activate(zz):
        gates = X[zz, :, :, 0, :, HALF:].reshape(128, 128).astype(F32)
        inv = jnp.sum(jnp.where(wide == 32, gates, 0.0), axis=1, keepdims=True)
        for e in range(2):
            weight = jnp.sum(jnp.where(wide == p * 2 + e, gates, 0.0), axis=1, keepdims=True)
            gu = GU[e, zz].reshape(128, 512) * inv
            act = jax.nn.silu(gu[:, :256]) * gu[:, 256:] * weight
            A[x, zz, :, :, e * 256 : e * 256 + 256] = act.astype(BF16).reshape(4, 32, 256)

    def act_ring(j):
        zz = (z + order[j]) % 4
        return Ring(
            28 + j, "x", lambda i: A.at[i, zz], lambda i: A.at[i, zz, pl.ds(0, 2)], lambda i: A.at[i, zz, pl.ds(2, 2)]
        )

    order = (2, 1, 3, 0)
    acts = [act_ring(j) for j in range(4)]
    over_y, over_z, last_z, last_y = [], [], [], []

    def down(j):
        zz = (z + order[j]) % 4
        for half, buf in ((1, Y1), (0, Y0)):
            acc = jnp.zeros((128, 896), F32)
            for i in range(4):
                acc += dot(A[i, zz].reshape(128, 512), WD[i, :, :, half * 896 : half * 896 + 896].reshape(512, 896))
            buf[j] = acc.reshape(4, 32, 896).astype(BF16)
            if half == 1 and j < 3:
                over_z.append(go(rcopy(Y1.at[j], R1.at[j], y1_s.at[j], y1_r.at[j], at(zz=zz))))
        group = []
        for m in range(3):
            yy = (y + order[m]) % 4
            group.append(go(rcopy(Y0.at[j, yy], R0.at[j, m], y0_s.at[j, m], y0_r.at[j, m], at(yy=yy))))
        over_y.append(group)

    def gather_y(j):
        zz = (z + order[j]) % 4
        for c in over_y[j]:
            c.wait_recv()
        acc = Y0[j, y].astype(F32)
        for m in range(3):
            acc += R0[j, m].astype(F32)
        if j < 3:
            T0[j] = acc.astype(BF16)
            last_z.append(go(rcopy(T0.at[j], Q0.at[j], y2_s.at[0, j], y2_r.at[0, j], at(zz=zz))))
        else:
            O0[...] = acc

    activate((z + order[0]) % 4)
    acts[0].start()
    activate((z + order[1]) % 4)
    acts[1].start()
    activate((z + order[2]) % 4)
    activate((z + order[3]) % 4)
    acts[0].forward()
    acts[2].start()
    for c in pass_on:
        c.wait_recv()
    acts[1].forward()
    acts[0].finish()
    acts[3].start()
    down(0)
    acts[2].forward()
    acts[1].finish()
    down(1)
    gather_y(0)
    acts[3].forward()
    acts[2].finish()
    down(2)
    gather_y(1)
    acts[3].finish()
    down(3)
    gather_y(2)
    for c in over_z:
        c.wait_recv()

    def sum_z(yy):
        acc = Y1[3, yy].astype(F32)
        for m in range(3):
            acc += R1[m, yy].astype(F32)
        return acc

    for m in range(3):
        yy = (y + order[m]) % 4
        T1[m] = sum_z(yy).astype(BF16)
        last_y.append(go(rcopy(T1.at[m], Q1.at[m], y2_s.at[1, m], y2_r.at[1, m], at(yy=yy))))
    gather_y(3)
    m0 = O0[...]
    m1 = sum_z(y)
    for c in to_out + last_z + last_y:
        c.wait_recv()
    for m in range(3):
        m0 += Q0[m].astype(F32)
        m1 += Q1[m].astype(F32)
    for r in range(2):
        rows = slice(r * 16, r * 16 + 16)
        low = jnp.concatenate([RL[r * 2 + h, i] for i in range(2) for h in range(2)], axis=1)
        high = jnp.concatenate([RL[r * 2 + h, i] for i in range(2, 4) for h in range(2)], axis=1)
        out_ref[rows, 0:896] = (low + m0[rows]).astype(BF16)
        out_ref[rows, 896:1792] = (high + m1[rows]).astype(BF16)

    for c in sends:
        c.wait_send()
    wgu_all.wait_send()
    lax.fori_loop(1, 64, partial_sent, 0)


def body(
    hidden_in, queries, latent_cache, new_latent, cache_lengths, value_up, out_proj, norm_gain, router, expert_ids,
    w_gate_up, w_down,
):
    wgu = w_gate_up[0].reshape(7168, 2, 2, 128).transpose(0, 2, 1, 3).reshape(28672, 128)
    any_spec = pl.BlockSpec(memory_space=pl.ANY)
    vmem = pl.BlockSpec(memory_space=pltpu.VMEM)
    dma = pltpu.SemaphoreType.DMA
    return pl.pallas_call(
        layer_kernel,
        out_shape=jax.ShapeDtypeStruct((32, 1792), BF16),
        in_specs=[any_spec] * 6 + [vmem] * 5 + [pl.BlockSpec(memory_space=pltpu.SMEM)],
        out_specs=vmem,
        scratch_shapes=[
            pltpu.VMEM((2, GROUP, 208, 576), BF16),
            pltpu.VMEM((32, 32, 576), BF16),
            pltpu.VMEM((32, 576), F32),
            pltpu.VMEM((4, 1024, 128), F32),
            pltpu.VMEM((32, 512, 128), BF16),
            pltpu.VMEM((2, 3584, 128), BF16),
            pltpu.VMEM((256, 256), BF16),
            pltpu.VMEM((16, 16, 224), F32),
            pltpu.VMEM((1, HALF), F32),
            pltpu.VMEM((128, HALF), BF16),
            pltpu.VMEM((16, 128), F32),
            pltpu.VMEM((4, 4, 32, 4096), BF16),
            pltpu.VMEM((2, 224, 4096), BF16),
            pltpu.VMEM((2, 4, 4, 32, 224), F32),
            pltpu.VMEM((4, 4, 4, 16, 224), BF16),
            pltpu.VMEM((4, 16, 16, 224), BF16),
            pltpu.VMEM((16, 128), F32),
            pltpu.VMEM((16, 128), F32),
            pltpu.VMEM((16, 16, 224), F32),
            pltpu.VMEM((4, 4, 16, 224), F32),
            pltpu.VMEM((4, 4, 2, 2, 16, 3712), BF16),
            pltpu.VMEM((2, 2, HALF, 512), BF16),
            pltpu.VMEM((2, 4, 4, 2, 16, 512), F32),
            pltpu.VMEM((4, 2, 256, 1792), BF16),
            pltpu.VMEM((4, 4, 4, 32, 512), BF16),
            pltpu.VMEM((4, 4, 32, 896), BF16),
            pltpu.VMEM((4, 4, 32, 896), BF16),
            pltpu.VMEM((4, 3, 32, 896), BF16),
            pltpu.VMEM((3, 4, 32, 896), BF16),
            pltpu.VMEM((3, 32, 896), BF16),
            pltpu.VMEM((3, 32, 896), BF16),
            pltpu.VMEM((3, 32, 896), BF16),
            pltpu.VMEM((3, 32, 896), BF16),
            pltpu.VMEM((32, 896), F32),
            dma((32, 4)),
            dma((32, 4)),
            dma((63,)),
            dma((63,)),
            dma((1,)),
            dma((1,)),
            dma((3,)),
            dma((3,)),
            dma((1,)),
            dma((1,)),
            dma((1,)),
            dma((1,)),
            dma((4,)),
            dma((4,)),
            dma((4,)),
            dma((4,)),
            dma((4, 3)),
            dma((4, 3)),
            dma((3,)),
            dma((3,)),
            dma((2, 3)),
            dma((2, 3)),
            dma((4,)),
            dma((2,)),
            dma((2,)),
        ],
        compiler_params=pltpu.CompilerParams(
            collective_id=0, has_side_effects=True, vmem_limit_bytes=66_000_000
        ),
        name="layer",
    )(
        queries, latent_cache, value_up, out_proj.T, wgu, w_down[0], new_latent, hidden_in, norm_gain.reshape(1, -1),
        router.T, expert_ids.T, cache_lengths,
    )


def solution(mesh):
    in_specs = (
        P("batch", None),
        P("batch", ("sec", "head"), None),
        P("batch", None, None),
        P("batch", None),
        P("batch"),
        P(("sec", "head"), None, None),
        P(("sec", "head"), "batch"),
        P(),
        P(),
        P("batch", None),
        P("batch", None, None, ("sec", "head")),
        P("batch", ("sec", "head"), None),
    )
    out_specs = P("batch", ("sec", "head"))
    return jax.shard_map(body, mesh=mesh, in_specs=in_specs, out_specs=out_specs, check_vma=False)
```

```python
import jax
import jax.numpy as jnp
from jax import lax
from jax.experimental import pallas as pl
from jax.experimental.pallas import tpu as pltpu
from jax.sharding import PartitionSpec as P

QKD = 192
TOP = 8
norm_epsilon = 1e-06
route_scale = 2.5

BF16, F32 = jnp.bfloat16, jnp.float32
MESH = pl.DeviceIdType.MESH
PARTS = ((0, 768, 1408), (1408, 1920, 2304), (2304, 3072, 3712))
HALF = 3584
GROUP = 8


def dot(a, b):
    return lax.dot_general(a, b, (((1,), (0,)), ((), ())), preferred_element_type=F32)


def dot_t(a, b):
    return lax.dot_general(a, b, (((1,), (1,)), ((), ())), preferred_element_type=F32)


def layer_kernel(
    q_hbm, cache_hbm, vu_hbm, wo_hbm, wgu_hbm, wd_hbm, new_ref, hidden_ref, gain_ref, router_ref, ids_ref, len_ref,
    out_ref,
    CA, Q, NEW, L, VU, RAW, PERM, HID, GAIN, ROUT, HIT,
    H, WO, ACC, PS, RX, SS, RY, MS, MR, RF, RL, X, WGU, GU, WD, A, Y0, Y1, R0, R1, T0, T1, Q0, Q1, O0,
    ring_s, ring_r, bx_s, bx_r, by_s, by_r, m_s, m_r, rl_s, rl_r, wo_s, wo_r, wg_s, wg_r, wd_s, wd_r, wf_s, wf_r,
    y0_s, y0_r, y1_s, y1_r, y2_s, y2_r, loc, ca_sem, raw_sem,
):
    sec = lax.axis_index("sec")
    head = lax.axis_index("head")
    batch = lax.axis_index("batch")
    core = batch % 2
    y = (batch // 2) % 4
    z = batch // 8
    x = head * 2 + sec
    p = z * 4 + y

    def at(zz=None, yy=None, cc=None, xx=None):
        zz = z if zz is None else zz
        yy = y if yy is None else yy
        cc = core if cc is None else cc
        xx = x if xx is None else xx
        return (xx % 2, zz * 8 + yy * 2 + cc, xx // 2)

    barrier = pltpu.get_barrier_semaphore()

    def greet(to):
        pl.semaphore_signal(barrier, inc=1, device_id=to, device_id_type=MESH)

    greet(at(cc=1 - core))
    for d in range(1, 4):
        greet(at(xx=(x + d) % 4))
    for d in range(1, 16):
        q = (p + d) % 16
        greet(at(zz=q // 4, yy=q % 4))

    def rcopy(src, dst, send, recv, to):
        return pltpu.make_async_remote_copy(
            src_ref=src, dst_ref=dst, send_sem=send, recv_sem=recv, device_id=to, device_id_type=MESH
        )

    def lcopy(src, dst, k):
        return pltpu.make_async_copy(src, dst, loc.at[k])

    sends = []

    def go(copy):
        copy.start()
        sends.append(copy)
        return copy

    def cache_copy(g, slot):
        return pltpu.make_async_copy(
            cache_hbm.at[pl.ds(g * GROUP, GROUP)], CA.at[slot, :, pl.ds(0, 192)], ca_sem.at[slot]
        )

    def raw_copy(i, slot):
        rows = pl.ds(pl.multiple_of(i * 3584, 128), 3584)
        return pltpu.make_async_copy(wgu_hbm.at[rows], RAW.at[slot], raw_sem.at[slot])

    own_q = lcopy(q_hbm, Q, 0)
    own_q.start()
    cache_copy(0, 0).start()
    cache_copy(1, 1).start()
    own_vu = lcopy(vu_hbm, VU, 2)
    own_vu.start()
    own_wo = lcopy(wo_hbm, WO.at[core], 1)
    own_wo.start()

    def wd_cols(xx):
        s = (xx % 2) * 2 + xx // 2
        return wd_hbm.at[:, pl.ds(pl.multiple_of(s * 1792, 128), 1792)]

    NEW[...] = new_ref[...].astype(F32)
    own_q.wait()
    pl.semaphore_wait(barrier, 19)

    other_core = at(cc=1 - core)
    send_wo = go(rcopy(wo_hbm, WO.at[core], wo_s.at[0], wo_r.at[0], other_core))
    send_wd = []
    for d in (1, 3):
        xx = (x + d) % 4
        send_wd.append(go(rcopy(wd_cols(xx), WD.at[x, core], wd_s.at[d - 1], wd_r.at[d - 1], at(xx=xx))))
    opposite = (x + 2) % 4

    def far_wd(k, rows):
        src, dst = wd_cols(opposite).at[rows], WD.at[x, core, rows]
        send_wd.append(go(rcopy(src, dst, wd_s.at[k], wd_r.at[k], at(xx=opposite))))

    far_wd(1, pl.ds(0, 128))

    own_row = lax.broadcasted_iota(jnp.int32, (16, 576), 0) == 0
    column = lax.broadcasted_iota(jnp.int32, (GROUP * 32, 208), 1)

    def attend(g, carry):
        slot = g % 2
        cache_copy(g, slot).wait()
        news = [NEW[pl.ds(g * GROUP + i, 1), :] for i in range(GROUP)]
        for i in range(GROUP):
            CA[slot, i, 192:208, :] = jnp.where(own_row, news[i], 0.0).astype(BF16)
        lengths = jnp.concatenate([jnp.full((32, 1), len_ref[g * GROUP + i], jnp.int32) for i in range(GROUP)], axis=0)
        scores = jnp.concatenate([dot_t(Q[g * GROUP + i], CA[slot, i]) for i in range(GROUP)], axis=0) * (QKD**-0.5)
        scores = jnp.where((column < lengths) | (column == 192), scores, -jnp.inf)
        weights = jnp.exp(scores - jnp.max(scores, axis=1, keepdims=True))
        weights = (weights / jnp.sum(weights, axis=1, keepdims=True)).astype(BF16)
        for i in range(GROUP):
            rows = pl.ds(pl.multiple_of((g * GROUP + i) * 32, 32), 32)
            latent = dot(weights[i * 32 : i * 32 + 32], CA[slot, i, :, 0:512])
            for c in range(4):
                L[c, rows, :] = latent[:, c * 128 : c * 128 + 128]

        @pl.when(g + 2 < 32 // GROUP)
        def _():
            cache_copy(g + 2, slot).start()

        return carry

    lax.fori_loop(0, 16 // GROUP, attend, 0)
    raw_copy(0, 0).start()
    raw_copy(1, 1).start()
    own_wd = lcopy(wd_cols(x), WD.at[x, core], 3)
    own_wd.start()
    own_vu.wait()

    def head_values(half):
        rows = pl.ds(half * 16, 16)

        def step(i, carry):
            for j in range(4):
                h = i * 4 + j
                parts = [L[c, pl.ds(half * 512 + h, 16, stride=32), :] for c in range(4)]
                latent = jnp.concatenate(parts, axis=1).astype(BF16)
                H[z, y, rows, pl.ds(pl.multiple_of(h * 128, 128), 128)] = dot(latent, VU[h]).astype(BF16)
            return carry

        return step

    dims = {"z": z, "y": y, "x": x}

    def neighbour(dim, d):
        i = (dims[dim] + d) % 4
        return at(zz=i) if dim == "z" else at(yy=i) if dim == "y" else at(xx=i)

    class Ring:
        def __init__(self, k, dim, full, low, high):
            self.k, self.dim, self.full, self.low, self.high = k, dim, full, low, high

        def copy(self, part, i, d, j):
            i = (dims[self.dim] + i) % 4
            return rcopy(part(i), part(i), ring_s.at[self.k, j], ring_r.at[self.k, j], neighbour(self.dim, d))

        def start(self):
            self.up = go(self.copy(self.full, 0, 1, 0))
            self.down = go(self.copy(self.full, 0, 3, 1))

        def forward(self):
            self.up.wait_recv()
            self.far_up = go(self.copy(self.low, 3, 1, 2))
            self.down.wait_recv()
            self.far_down = go(self.copy(self.high, 1, 3, 3))

        def finish(self):
            self.far_up.wait_recv()
            self.far_down.wait_recv()

    def head_ring(k, dim, half, other, low):
        def view(first, count):
            def part(i):
                cols = pl.ds(half * 2048 + first, count)
                rows = pl.ds(low * 16, 16)
                if dim == "z":
                    return H.at[i, (y + other) % 4, rows, cols]
                return H.at[(z + other) % 4, i, rows, cols]

            return part

        return Ring(k, dim, view(0, 2048), view(0, 1024), view(1024, 1024))

    near, wide_rings = [], []
    for low in range(2):
        k = low * 10
        near.append((head_ring(k, "y", 0, 0, low), head_ring(k + 1, "z", 1, 0, low)))
        wide_rings.append(
            [(head_ring(k + 2 + o, "z", 0, o, low), head_ring(k + 6 + o, "y", 1, o, low)) for o in range(4)]
        )

    def start_rows(low, half):
        near[low][half].start()
        wide_rings[low][0][half].start()

    def near_forward(low):
        for half in range(2):
            near[low][half].forward()
        for o in (1, 3):
            for half in range(2):
                wide_rings[low][o][half].start()

    def near_finish(low):
        for half in range(2):
            wide_rings[low][0][half].forward()
        for half in range(2):
            near[low][half].finish()
            wide_rings[low][2][half].start()

    def wide_forward(low, o):
        for half in range(2):
            wide_rings[low][o][half].forward()

    lax.fori_loop(0, 4, head_values(0), 0)
    start_rows(0, 0)
    lax.fori_loop(4, 8, head_values(0), 0)
    start_rows(0, 1)
    lax.fori_loop(16 // GROUP, 32 // GROUP, attend, 0)
    near_forward(0)
    lax.fori_loop(0, 4, head_values(1), 0)
    start_rows(1, 0)
    lax.fori_loop(4, 8, head_values(1), 0)
    start_rows(1, 1)
    near_finish(0)

    spread_row = lax.broadcasted_iota(jnp.int32, (256, 256), 0)
    spread_col = lax.broadcasted_iota(jnp.int32, (256, 256), 1)
    PERM[...] = jnp.where(spread_col == (spread_row % 64) * 4 + spread_row // 64, 1.0, 0.0).astype(BF16)

    def separate(i, carry):
        slot = i % 2
        raw_copy(i, slot).wait()
        for b in range(0, 14, 2):
            pair = jnp.concatenate([RAW[slot, b * 256 : b * 256 + 256], RAW[slot, b * 256 + 256 : b * 256 + 512]], axis=1)
            moved = dot(PERM[...], pair).astype(BF16)
            for j in range(2):
                for u in range(2):
                    k = (b + j) * 64 + u * 32
                    h, row = (k // 224) % 2, k // 448 * 224 + k % 224
                    row = pl.multiple_of(i * 448 + row, 32)
                    for q in range(4):
                        to = q % 2 * 256 + q // 2 * 128
                        a = q * 64 + u * 32
                        WGU[core, h, pl.ds(row, 32), to : to + 128] = moved[a : a + 32, j * 128 : j * 128 + 128]

        @pl.when(i + 2 < 8)
        def _():
            raw_copy(i + 2, slot).start()

        return carry

    def far_wgu(i, h):
        block = WGU.at[core, h, pl.ds(i * 448, 448)]
        return rcopy(block, block, wg_s.at[0], wg_r.at[0], other_core)

    wgu_all = rcopy(WGU.at[core], WGU.at[core], wg_s.at[0], wg_r.at[0], other_core)

    def pieces(v):
        return [jnp.where(sec == 0, v[:, i * 448 : i * 448 + 224], v[:, i * 448 + 224 : i * 448 + 448]) for i in range(16)]

    def pack_inputs():
        for i, piece in enumerate(pieces(hidden_ref[pl.ds(pl.multiple_of(head * 16, 16), 16), :].astype(F32))):
            HID[i] = piece
        GAIN[...] = jnp.concatenate(pieces(gain_ref[...]), axis=1)
        ROUT[0:32, :] = jnp.concatenate(pieces(router_ref[...].astype(F32)), axis=1).astype(BF16)
        ROUT[32:128, :] = jnp.zeros((96, HALF), BF16)
        expert = lax.broadcasted_iota(jnp.int32, (128, 32), 0)
        hit = jnp.zeros((128, 32), F32)
        for k in range(TOP):
            hit += jnp.where(ids_ref[k : k + 1, :] == expert, 1.0, 0.0)
        mine = lax.broadcasted_iota(jnp.int32, (16, 32), 1) == lax.broadcasted_iota(jnp.int32, (16, 32), 0) + head * 16
        HIT[...] = dot_t(jnp.where(mine, 1.0, 0.0).astype(BF16), hit.astype(BF16))

    ACC[...] = jnp.zeros_like(ACC)
    lax.fori_loop(0, 1, separate, 0)
    near_forward(1)
    lax.fori_loop(1, 2, separate, 0)
    wide_forward(0, 1)
    wide_forward(0, 3)
    near_finish(1)
    lax.fori_loop(2, 4, separate, 0)
    wide_forward(0, 2)
    for i in range(4):
        for h in range(2):
            far_wgu(i, h).start()
    lax.fori_loop(4, 7, separate, 0)
    wide_forward(1, 1)
    wide_forward(1, 3)
    lax.fori_loop(7, 8, separate, 0)
    pack_inputs()
    for i in range(4, 8):
        for h in range(2):
            far_wgu(i, h).start()

    own_wo.wait()
    send_wo.wait_recv()

    def project_z(zz):
        rows = H[zz, :, :, 0:2048].reshape(128, 2048)
        for n in range(2):
            ACC[n, zz] += dot_t(rows, WO[n, :, 0:2048]).reshape(4, 32, 224)

    def project_y(yy):
        rows = H[:, yy, :, 2048:4096].reshape(128, 2048)
        for n in range(2):
            ACC[n, :, yy] += dot_t(rows, WO[n, :, 2048:4096]).reshape(4, 32, 224)

    def project(d):
        project_z((z + d) % 4)
        project_y((y + d) % 4)

    project(0)
    wide_forward(1, 2)
    project(1)
    project(3)
    for low in range(2):
        for o in range(4):
            for half in range(2):
                wide_rings[low][o][half].finish()
    project(2)

    for r in range(2):
        for h in range(2):
            PS[r * 2 + h] = ACC[h, :, :, r * 16 : r * 16 + 16, :].astype(BF16)
    cross = []
    for d in (2, 1, 3):
        xx = (x + d) % 4
        cross.append(go(rcopy(PS.at[xx], RX.at[x], bx_s.at[d - 1], bx_r.at[d - 1], at(xx=xx))))
    far_wd(3, pl.ds(128, 128))
    for c in cross:
        c.wait_recv()
    total = PS[x].astype(F32)
    for d in range(1, 4):
        total += RX[(x + d) % 4].astype(F32)
    SS[...] = total.astype(BF16)
    plane = []
    for d in range(1, 16):
        q = (p + d) % 16
        plane.append(go(rcopy(SS.at[q // 4, q % 4], RY.at[p], by_s.at[d - 1], by_r.at[d - 1], at(zz=q // 4, yy=q % 4))))
    RY[p] = SS[z, y]
    for c in plane:
        c.wait_recv()

    RF[...] = RY[...].astype(F32) + HID[...]
    res = jnp.concatenate([RF[i] for i in range(16)], axis=1)
    scaled = res * GAIN[...]
    lane = lax.broadcasted_iota(jnp.int32, (16, 128), 1)
    square = jnp.sum(res * res, axis=1, keepdims=True)
    note = dot_t(scaled.astype(BF16), ROUT[...])
    MS[...] = jnp.where(lane == 32, square, note)
    X[z, y, head, sec, :, 0:HALF] = scaled.astype(BF16)
    msg = go(rcopy(MS, MR, m_s.at[0], m_r.at[0], at(xx=x + 1 - 2 * sec)))
    def row_ring(k, part, dim, done, fixed):
        c0, c1, c2 = PARTS[part]

        def view(a, b):
            def block(i):
                at_dim = {}
                for d in "zyx":
                    at_dim[d] = i if d == dim else None if d in done else (dims[d] + fixed.get(d, 0)) % 4
                zi, yi, xi = (slice(None) if at_dim[d] is None else at_dim[d] for d in "zyx")
                if at_dim["x"] is None:
                    return X.at[zi, yi, :, :, :, pl.ds(a, b - a)]
                return X.at[zi, yi, xi // 2, xi % 2, :, pl.ds(a, b - a)]

            return block

        return Ring(k, dim, view(c0, c2), view(c0, c1), view(c1, c2))

    first, second, third = [], [], []
    for part, (d1, d2, d3) in enumerate(("xyz", "yzx", "zxy")):
        first.append(row_ring(20 + part, part, d1, "", {}))
        second.append(row_ring(23 + part, part, d2, d1, {}))
        third.append([row_ring(26 + part * 4 + o, part, d3, d1, {d2: o}) for o in range(4)])
    GU[...] = jnp.zeros_like(GU)
    first[0].start()
    first[1].start()

    msg.wait_recv()
    both = MS[...] + MR[...]
    mean_square = jnp.sum(jnp.where(lane == 32, both, 0.0), axis=1, keepdims=True) / (2 * HALF)
    inv = lax.rsqrt(mean_square + norm_epsilon)
    affinity = jax.nn.sigmoid(both * inv)
    picked = jnp.where(HIT[...] > 0.0, affinity, 0.0)
    gate = route_scale * picked / jnp.sum(picked, axis=1, keepdims=True)
    gate = jnp.where(lane == 32, inv, gate)
    top = gate.astype(BF16).astype(F32)
    X[z, y, head, sec, :, HALF:] = (top + pltpu.roll(gate - top, 64, 1)).astype(BF16)
    first[2].start()

    for ring in first:
        ring.forward()
    for before, ring in zip(first, second):
        before.finish()
        ring.start()
    for rings in third:
        rings[0].start()
    for ring in second:
        ring.forward()
    for rings in third:
        rings[1].start()
        rings[3].start()

    to_out = []
    for d in range(1, 4):
        xx = (x + d) % 4
        s = (xx % 2) * 2 + xx // 2
        to_out.append(go(rcopy(RF.at[pl.ds(s * 4, 4)], RL.at[x], rl_s.at[d - 1], rl_r.at[d - 1], at(xx=xx))))
    RL[x] = RF[pl.ds((sec * 2 + head) * 4, 4)]
    for rings in third:
        rings[0].forward()
    for before, rings in zip(second, third):
        before.finish()
        rings[2].start()

    for c in send_wd:
        c.wait_recv()
    own_wd.wait()

    pass_on = []
    for i in range(4):
        pass_on.append(go(rcopy(WD.at[i, core], WD.at[i, core], wf_s.at[i], wf_r.at[i], other_core)))
    wgu_all.wait_recv()

    def cols(part):
        return PARTS[part][0], min(PARTS[part][2], HALF)

    def experts_z(zz):
        a, b = cols(0)
        for h in range(2):
            rows = X[zz, :, :, h, :, a:b].reshape(128, b - a)
            for e in range(2):
                GU[e, zz] += dot(rows, WGU[e, h, a:b]).reshape(4, 2, 16, 512)

    def experts_x(xx):
        a, b = cols(1)
        r, h = xx // 2, xx % 2
        rows = X[:, :, r, h, :, a:b].reshape(256, b - a)
        for e in range(2):
            GU[e, :, :, r] += dot(rows, WGU[e, h, a:b]).reshape(4, 4, 16, 512)

    def experts_y(yy):
        a, b = cols(2)
        for h in range(2):
            rows = X[:, yy, :, h, :, a:b].reshape(128, b - a)
            for e in range(2):
                GU[e, :, yy] += dot(rows, WGU[e, h, a:b]).reshape(4, 2, 16, 512)

    def experts(d):
        experts_z((z + d) % 4)
        experts_x((x + d) % 4)
        experts_y((y + d) % 4)

    experts(0)
    for o in (1, 3, 2):
        for rings in third:
            rings[o].forward()
    experts(1)
    experts(3)
    for o in range(4):
        for rings in third:
            rings[o].finish()
    experts(2)

    wide = lax.broadcasted_iota(jnp.int32, (128, 128), 1) % 64

    def activate(zz):
        gates = X[zz, :, :, 0, :, HALF:].reshape(128, 128).astype(F32)
        inv = jnp.sum(jnp.where(wide == 32, gates, 0.0), axis=1, keepdims=True)
        for e in range(2):
            weight = jnp.sum(jnp.where(wide == p * 2 + e, gates, 0.0), axis=1, keepdims=True)
            gu = GU[e, zz].reshape(128, 512) * inv
            act = jax.nn.silu(gu[:, :256]) * gu[:, 256:] * weight
            A[x, zz, :, :, e * 256 : e * 256 + 256] = act.astype(BF16).reshape(4, 32, 256)

    def act_ring(j):
        zz = (z + order[j]) % 4
        return Ring(
            38 + j, "x", lambda i: A.at[i, zz], lambda i: A.at[i, zz, pl.ds(0, 2)], lambda i: A.at[i, zz, pl.ds(2, 2)]
        )

    order = (2, 1, 3, 0)
    acts = [act_ring(j) for j in range(4)]
    over_y, over_z, last_z, last_y = [], [], [], []

    def down(j):
        zz = (z + order[j]) % 4
        for half, buf in ((1, Y1), (0, Y0)):
            acc = jnp.zeros((128, 896), F32)
            for i in range(4):
                acc += dot(A[i, zz].reshape(128, 512), WD[i, :, :, half * 896 : half * 896 + 896].reshape(512, 896))
            buf[j] = acc.reshape(4, 32, 896).astype(BF16)
            if half == 1 and j < 3:
                over_z.append(go(rcopy(Y1.at[j], R1.at[j], y1_s.at[j], y1_r.at[j], at(zz=zz))))
        group = []
        for m in range(3):
            yy = (y + order[m]) % 4
            group.append(go(rcopy(Y0.at[j, yy], R0.at[j, m], y0_s.at[j, m], y0_r.at[j, m], at(yy=yy))))
        over_y.append(group)

    def gather_y(j):
        zz = (z + order[j]) % 4
        for c in over_y[j]:
            c.wait_recv()
        acc = Y0[j, y].astype(F32)
        for m in range(3):
            acc += R0[j, m].astype(F32)
        if j < 3:
            T0[j] = acc.astype(BF16)
            last_z.append(go(rcopy(T0.at[j], Q0.at[j], y2_s.at[0, j], y2_r.at[0, j], at(zz=zz))))
        else:
            O0[...] = acc

    activate((z + order[0]) % 4)
    acts[0].start()
    activate((z + order[1]) % 4)
    acts[1].start()
    activate((z + order[2]) % 4)
    activate((z + order[3]) % 4)
    acts[0].forward()
    acts[2].start()
    for c in pass_on:
        c.wait_recv()
    acts[1].forward()
    acts[0].finish()
    acts[3].start()
    down(0)
    acts[2].forward()
    acts[1].finish()
    down(1)
    gather_y(0)
    acts[3].forward()
    acts[2].finish()
    down(2)
    gather_y(1)
    acts[3].finish()
    down(3)
    gather_y(2)
    for c in over_z:
        c.wait_recv()

    def sum_z(yy):
        acc = Y1[3, yy].astype(F32)
        for m in range(3):
            acc += R1[m, yy].astype(F32)
        return acc

    for m in range(3):
        yy = (y + order[m]) % 4
        T1[m] = sum_z(yy).astype(BF16)
        last_y.append(go(rcopy(T1.at[m], Q1.at[m], y2_s.at[1, m], y2_r.at[1, m], at(yy=yy))))
    gather_y(3)
    m0 = O0[...]
    m1 = sum_z(y)
    for c in to_out + last_z + last_y:
        c.wait_recv()
    for m in range(3):
        m0 += Q0[m].astype(F32)
        m1 += Q1[m].astype(F32)
    for r in range(2):
        rows = slice(r * 16, r * 16 + 16)
        low = jnp.concatenate([RL[r * 2 + h, i] for i in range(2) for h in range(2)], axis=1)
        high = jnp.concatenate([RL[r * 2 + h, i] for i in range(2, 4) for h in range(2)], axis=1)
        out_ref[rows, 0:896] = (low + m0[rows]).astype(BF16)
        out_ref[rows, 896:1792] = (high + m1[rows]).astype(BF16)

    for c in sends:
        c.wait_send()
    wgu_all.wait_send()


def body(
    hidden_in, queries, latent_cache, new_latent, cache_lengths, value_up, out_proj, norm_gain, router, expert_ids,
    w_gate_up, w_down,
):
    wgu = w_gate_up[0].reshape(7168, 2, 2, 128).transpose(0, 2, 1, 3).reshape(28672, 128)
    any_spec = pl.BlockSpec(memory_space=pl.ANY)
    vmem = pl.BlockSpec(memory_space=pltpu.VMEM)
    dma = pltpu.SemaphoreType.DMA
    return pl.pallas_call(
        layer_kernel,
        out_shape=jax.ShapeDtypeStruct((32, 1792), BF16),
        in_specs=[any_spec] * 6 + [vmem] * 5 + [pl.BlockSpec(memory_space=pltpu.SMEM)],
        out_specs=vmem,
        scratch_shapes=[
            pltpu.VMEM((2, GROUP, 208, 576), BF16),
            pltpu.VMEM((32, 32, 576), BF16),
            pltpu.VMEM((32, 576), F32),
            pltpu.VMEM((4, 1024, 128), F32),
            pltpu.VMEM((32, 512, 128), BF16),
            pltpu.VMEM((2, 3584, 128), BF16),
            pltpu.VMEM((256, 256), BF16),
            pltpu.VMEM((16, 16, 224), F32),
            pltpu.VMEM((1, HALF), F32),
            pltpu.VMEM((128, HALF), BF16),
            pltpu.VMEM((16, 128), F32),
            pltpu.VMEM((4, 4, 32, 4096), BF16),
            pltpu.VMEM((2, 224, 4096), BF16),
            pltpu.VMEM((2, 4, 4, 32, 224), F32),
            pltpu.VMEM((4, 4, 4, 16, 224), BF16),
            pltpu.VMEM((4, 4, 4, 16, 224), BF16),
            pltpu.VMEM((4, 4, 16, 224), BF16),
            pltpu.VMEM((16, 16, 224), BF16),
            pltpu.VMEM((16, 128), F32),
            pltpu.VMEM((16, 128), F32),
            pltpu.VMEM((16, 16, 224), F32),
            pltpu.VMEM((4, 4, 16, 224), F32),
            pltpu.VMEM((4, 4, 2, 2, 16, 3712), BF16),
            pltpu.VMEM((2, 2, HALF, 512), BF16),
            pltpu.VMEM((2, 4, 4, 2, 16, 512), F32),
            pltpu.VMEM((4, 2, 256, 1792), BF16),
            pltpu.VMEM((4, 4, 4, 32, 512), BF16),
            pltpu.VMEM((4, 4, 32, 896), BF16),
            pltpu.VMEM((4, 4, 32, 896), BF16),
            pltpu.VMEM((4, 3, 32, 896), BF16),
            pltpu.VMEM((3, 4, 32, 896), BF16),
            pltpu.VMEM((3, 32, 896), BF16),
            pltpu.VMEM((3, 32, 896), BF16),
            pltpu.VMEM((3, 32, 896), BF16),
            pltpu.VMEM((3, 32, 896), BF16),
            pltpu.VMEM((32, 896), F32),
            dma((42, 4)),
            dma((42, 4)),
            dma((3,)),
            dma((3,)),
            dma((15,)),
            dma((15,)),
            dma((1,)),
            dma((1,)),
            dma((3,)),
            dma((3,)),
            dma((1,)),
            dma((1,)),
            dma((1,)),
            dma((1,)),
            dma((4,)),
            dma((4,)),
            dma((4,)),
            dma((4,)),
            dma((4, 3)),
            dma((4, 3)),
            dma((3,)),
            dma((3,)),
            dma((2, 3)),
            dma((2, 3)),
            dma((4,)),
            dma((2,)),
            dma((2,)),
        ],
        compiler_params=pltpu.CompilerParams(
            collective_id=0, has_side_effects=True, vmem_limit_bytes=66_000_000
        ),
        name="layer",
    )(
        queries, latent_cache, value_up, out_proj.T, wgu, w_down[0], new_latent, hidden_in, norm_gain.reshape(1, -1),
        router.T, expert_ids.T, cache_lengths,
    )


def solution(mesh):
    in_specs = (
        P("batch", None),
        P("batch", ("sec", "head"), None),
        P("batch", None, None),
        P("batch", None),
        P("batch"),
        P(("sec", "head"), None, None),
        P(("sec", "head"), "batch"),
        P(),
        P(),
        P("batch", None),
        P("batch", None, None, ("sec", "head")),
        P("batch", ("sec", "head"), None),
    )
    out_specs = P("batch", ("sec", "head"))
    return jax.shard_map(body, mesh=mesh, in_specs=in_specs, out_specs=out_specs, check_vma=False)
```

```python
import jax
import jax.numpy as jnp
from jax import lax
from jax.experimental import pallas as pl
from jax.experimental.pallas import tpu as pltpu
from jax.sharding import PartitionSpec as P

QKD = 192
TOP = 8
norm_epsilon = 1e-06
route_scale = 2.5

BF16, F32 = jnp.bfloat16, jnp.float32
MESH = pl.DeviceIdType.MESH
PARTS = ((0, 768, 1408), (1408, 1920, 2304), (2304, 3072, 3712))
HALF = 3584
GROUP = 8


def dot(a, b):
    return lax.dot_general(a, b, (((1,), (0,)), ((), ())), preferred_element_type=F32)


def dot_t(a, b):
    return lax.dot_general(a, b, (((1,), (1,)), ((), ())), preferred_element_type=F32)


def layer_kernel(
    q_hbm, cache_hbm, vu_hbm, wo_hbm, wgu_hbm, wd_hbm, new_ref, hidden_ref, gain_ref, router_ref, ids_ref, len_ref,
    out_ref,
    CA, Q, NEW, L, VU, RAW, PERM, HID, GAIN, ROUT, HIT,
    H, WO, ACC, PS, RX, SS, RY, MS, MR, RF, RL, X, WGU, GU, WD, A, Y0, Y1, R0, R1, T0, T1, Q0, Q1, O0,
    ring_s, ring_r, bx_s, bx_r, by_s, by_r, m_s, m_r, rl_s, rl_r, wo_s, wo_r, wg_s, wg_r, wd_s, wd_r, wf_s, wf_r,
    y0_s, y0_r, y1_s, y1_r, y2_s, y2_r, loc, ca_sem, raw_sem,
):
    sec = lax.axis_index("sec")
    head = lax.axis_index("head")
    batch = lax.axis_index("batch")
    core = batch % 2
    y = (batch // 2) % 4
    z = batch // 8
    x = head * 2 + sec
    p = z * 4 + y

    def at(zz=None, yy=None, cc=None, xx=None):
        zz = z if zz is None else zz
        yy = y if yy is None else yy
        cc = core if cc is None else cc
        xx = x if xx is None else xx
        return (xx % 2, zz * 8 + yy * 2 + cc, xx // 2)

    barrier = pltpu.get_barrier_semaphore()

    def greet(to):
        pl.semaphore_signal(barrier, inc=1, device_id=to, device_id_type=MESH)

    greet(at(cc=1 - core))
    for d in range(1, 4):
        greet(at(xx=(x + d) % 4))
    for d in range(1, 16):
        q = (p + d) % 16
        greet(at(zz=q // 4, yy=q % 4))

    def rcopy(src, dst, send, recv, to):
        return pltpu.make_async_remote_copy(
            src_ref=src, dst_ref=dst, send_sem=send, recv_sem=recv, device_id=to, device_id_type=MESH
        )

    def lcopy(src, dst, k):
        return pltpu.make_async_copy(src, dst, loc.at[k])

    sends = []

    def go(copy):
        copy.start()
        sends.append(copy)
        return copy

    def cache_copy(g, slot):
        return pltpu.make_async_copy(
            cache_hbm.at[pl.ds(g * GROUP, GROUP)], CA.at[slot, :, pl.ds(0, 192)], ca_sem.at[slot]
        )

    def raw_copy(i, slot):
        rows = pl.ds(pl.multiple_of(i * 3584, 128), 3584)
        return pltpu.make_async_copy(wgu_hbm.at[rows], RAW.at[slot], raw_sem.at[slot])

    own_q = lcopy(q_hbm, Q, 0)
    own_q.start()
    cache_copy(0, 0).start()
    cache_copy(1, 1).start()
    own_vu = lcopy(vu_hbm, VU, 2)
    own_vu.start()
    own_wo = lcopy(wo_hbm, WO.at[core], 1)
    own_wo.start()

    def wd_cols(xx):
        s = (xx % 2) * 2 + xx // 2
        return wd_hbm.at[:, pl.ds(pl.multiple_of(s * 1792, 128), 1792)]

    NEW[...] = new_ref[...].astype(F32)
    own_q.wait()
    pl.semaphore_wait(barrier, 19)

    other_core = at(cc=1 - core)
    send_wo = go(rcopy(wo_hbm, WO.at[core], wo_s.at[0], wo_r.at[0], other_core))
    send_wd = []
    for d in (1, 3):
        xx = (x + d) % 4
        send_wd.append(go(rcopy(wd_cols(xx), WD.at[x, core], wd_s.at[d - 1], wd_r.at[d - 1], at(xx=xx))))
    opposite = (x + 2) % 4

    def far_wd(k, rows):
        src, dst = wd_cols(opposite).at[rows], WD.at[x, core, rows]
        send_wd.append(go(rcopy(src, dst, wd_s.at[k], wd_r.at[k], at(xx=opposite))))

    far_wd(1, pl.ds(0, 128))

    own_row = lax.broadcasted_iota(jnp.int32, (16, 576), 0) == 0
    column = lax.broadcasted_iota(jnp.int32, (GROUP * 32, 208), 1)

    def attend(g, carry):
        slot = g % 2
        cache_copy(g, slot).wait()
        news = [NEW[pl.ds(g * GROUP + i, 1), :] for i in range(GROUP)]
        for i in range(GROUP):
            CA[slot, i, 192:208, :] = jnp.where(own_row, news[i], 0.0).astype(BF16)
        lengths = jnp.concatenate([jnp.full((32, 1), len_ref[g * GROUP + i], jnp.int32) for i in range(GROUP)], axis=0)
        scores = jnp.concatenate([dot_t(Q[g * GROUP + i], CA[slot, i]) for i in range(GROUP)], axis=0) * (QKD**-0.5)
        scores = jnp.where((column < lengths) | (column == 192), scores, -jnp.inf)
        weights = jnp.exp(scores - jnp.max(scores, axis=1, keepdims=True))
        weights = (weights / jnp.sum(weights, axis=1, keepdims=True)).astype(BF16)
        for i in range(GROUP):
            rows = pl.ds(pl.multiple_of((g * GROUP + i) * 32, 32), 32)
            latent = dot(weights[i * 32 : i * 32 + 32], CA[slot, i, :, 0:512])
            for c in range(4):
                L[c, rows, :] = latent[:, c * 128 : c * 128 + 128]

        @pl.when(g + 2 < 32 // GROUP)
        def _():
            cache_copy(g + 2, slot).start()

        return carry

    lax.fori_loop(0, 32 // GROUP, attend, 0)
    raw_copy(0, 0).start()
    raw_copy(1, 1).start()
    own_wd = lcopy(wd_cols(x), WD.at[x, core], 3)
    own_wd.start()
    own_vu.wait()

    def head_values(i, carry):
        for j in range(4):
            h = i * 4 + j
            latent = jnp.concatenate([L[c, pl.ds(h, 32, stride=32), :] for c in range(4)], axis=1).astype(BF16)
            H[z, y, :, pl.ds(pl.multiple_of(h * 128, 128), 128)] = dot(latent, VU[h]).astype(BF16)
        return carry

    dims = {"z": z, "y": y, "x": x}

    def neighbour(dim, d):
        i = (dims[dim] + d) % 4
        return at(zz=i) if dim == "z" else at(yy=i) if dim == "y" else at(xx=i)

    class Ring:
        def __init__(self, k, dim, full, low, high):
            self.k, self.dim, self.full, self.low, self.high = k, dim, full, low, high

        def copy(self, part, i, d, j):
            i = (dims[self.dim] + i) % 4
            return rcopy(part(i), part(i), ring_s.at[self.k, j], ring_r.at[self.k, j], neighbour(self.dim, d))

        def start(self):
            self.up = go(self.copy(self.full, 0, 1, 0))
            self.down = go(self.copy(self.full, 0, 3, 1))

        def forward(self):
            self.up.wait_recv()
            self.far_up = go(self.copy(self.low, 3, 1, 2))
            self.down.wait_recv()
            self.far_down = go(self.copy(self.high, 1, 3, 3))

        def finish(self):
            self.far_up.wait_recv()
            self.far_down.wait_recv()

    def head_ring(k, dim, half, other):
        def view(rows):
            def part(i):
                cols = pl.ds(half * 2048, 2048)
                if dim == "z":
                    return H.at[i, (y + other) % 4, rows, cols]
                return H.at[(z + other) % 4, i, rows, cols]

            return part

        return Ring(k, dim, view(pl.ds(0, 32)), view(pl.ds(0, 16)), view(pl.ds(16, 16)))

    h0a, h0b = head_ring(0, "y", 0, 0), [head_ring(1 + o, "z", 0, o) for o in range(4)]
    h1a, h1b = head_ring(5, "z", 1, 0), [head_ring(6 + o, "y", 1, o) for o in range(4)]

    lax.fori_loop(0, 4, head_values, 0)
    h0a.start()
    h0b[0].start()
    lax.fori_loop(4, 8, head_values, 0)
    h1a.start()
    h1b[0].start()

    spread_row = lax.broadcasted_iota(jnp.int32, (256, 256), 0)
    spread_col = lax.broadcasted_iota(jnp.int32, (256, 256), 1)
    PERM[...] = jnp.where(spread_col == (spread_row % 64) * 4 + spread_row // 64, 1.0, 0.0).astype(BF16)

    def separate(i, carry):
        slot = i % 2
        raw_copy(i, slot).wait()
        for b in range(0, 14, 2):
            pair = jnp.concatenate([RAW[slot, b * 256 : b * 256 + 256], RAW[slot, b * 256 + 256 : b * 256 + 512]], axis=1)
            moved = dot(PERM[...], pair).astype(BF16)
            for j in range(2):
                for u in range(2):
                    k = (b + j) * 64 + u * 32
                    h, row = (k // 224) % 2, k // 448 * 224 + k % 224
                    row = pl.multiple_of(i * 448 + row, 32)
                    for q in range(4):
                        to = q % 2 * 256 + q // 2 * 128
                        a = q * 64 + u * 32
                        WGU[core, h, pl.ds(row, 32), to : to + 128] = moved[a : a + 32, j * 128 : j * 128 + 128]

        @pl.when(i + 2 < 8)
        def _():
            raw_copy(i + 2, slot).start()

        return carry

    def far_wgu(i, h):
        block = WGU.at[core, h, pl.ds(i * 448, 448)]
        return rcopy(block, block, wg_s.at[0], wg_r.at[0], other_core)

    wgu_all = rcopy(WGU.at[core], WGU.at[core], wg_s.at[0], wg_r.at[0], other_core)

    def pieces(v):
        return [jnp.where(sec == 0, v[:, i * 448 : i * 448 + 224], v[:, i * 448 + 224 : i * 448 + 448]) for i in range(16)]

    def pack_inputs():
        for i, piece in enumerate(pieces(hidden_ref[pl.ds(pl.multiple_of(head * 16, 16), 16), :].astype(F32))):
            HID[i] = piece
        GAIN[...] = jnp.concatenate(pieces(gain_ref[...]), axis=1)
        ROUT[0:32, :] = jnp.concatenate(pieces(router_ref[...].astype(F32)), axis=1).astype(BF16)
        ROUT[32:128, :] = jnp.zeros((96, HALF), BF16)
        expert = lax.broadcasted_iota(jnp.int32, (128, 32), 0)
        hit = jnp.zeros((128, 32), F32)
        for k in range(TOP):
            hit += jnp.where(ids_ref[k : k + 1, :] == expert, 1.0, 0.0)
        mine = lax.broadcasted_iota(jnp.int32, (16, 32), 1) == lax.broadcasted_iota(jnp.int32, (16, 32), 0) + head * 16
        HIT[...] = dot_t(jnp.where(mine, 1.0, 0.0).astype(BF16), hit.astype(BF16))

    ACC[...] = jnp.zeros_like(ACC)
    lax.fori_loop(0, 1, separate, 0)
    h0a.forward()
    h1a.forward()
    for o in (1, 3):
        h0b[o].start()
        h1b[o].start()
    lax.fori_loop(1, 2, separate, 0)
    h0b[0].forward()
    h1b[0].forward()
    h0a.finish()
    h0b[2].start()
    h1a.finish()
    h1b[2].start()
    lax.fori_loop(2, 4, separate, 0)
    for i in range(4):
        for h in range(2):
            far_wgu(i, h).start()
    lax.fori_loop(4, 7, separate, 0)
    for o in (1, 3):
        h0b[o].forward()
        h1b[o].forward()
    lax.fori_loop(7, 8, separate, 0)
    pack_inputs()
    for i in range(4, 8):
        for h in range(2):
            far_wgu(i, h).start()

    own_wo.wait()
    send_wo.wait_recv()

    def project_z(zz):
        rows = H[zz, :, :, 0:2048].reshape(128, 2048)
        for n in range(2):
            ACC[n, zz] += dot_t(rows, WO[n, :, 0:2048]).reshape(4, 32, 224)

    def project_y(yy):
        rows = H[:, yy, :, 2048:4096].reshape(128, 2048)
        for n in range(2):
            ACC[n, :, yy] += dot_t(rows, WO[n, :, 2048:4096]).reshape(4, 32, 224)

    def project(d):
        project_z((z + d) % 4)
        project_y((y + d) % 4)

    project(0)
    h0b[2].forward()
    h1b[2].forward()
    project(1)
    project(3)
    for o in range(4):
        h0b[o].finish()
        h1b[o].finish()
    project(2)

    for r in range(2):
        for h in range(2):
            PS[r * 2 + h] = ACC[h, :, :, r * 16 : r * 16 + 16, :].astype(BF16)
    cross = []
    for d in (2, 1, 3):
        xx = (x + d) % 4
        cross.append(go(rcopy(PS.at[xx], RX.at[x], bx_s.at[d - 1], bx_r.at[d - 1], at(xx=xx))))
    far_wd(3, pl.ds(128, 64))
    for c in cross:
        c.wait_recv()
    total = PS[x].astype(F32)
    for d in range(1, 4):
        total += RX[(x + d) % 4].astype(F32)
    SS[...] = total.astype(BF16)
    plane = []
    for d in range(1, 16):
        q = (p + d) % 16
        plane.append(go(rcopy(SS.at[q // 4, q % 4], RY.at[p], by_s.at[d - 1], by_r.at[d - 1], at(zz=q // 4, yy=q % 4))))
    RY[p] = SS[z, y]
    for c in plane:
        c.wait_recv()

    RF[...] = RY[...].astype(F32) + HID[...]
    res = jnp.concatenate([RF[i] for i in range(16)], axis=1)
    scaled = res * GAIN[...]
    lane = lax.broadcasted_iota(jnp.int32, (16, 128), 1)
    square = jnp.sum(res * res, axis=1, keepdims=True)
    note = dot_t(scaled.astype(BF16), ROUT[...])
    MS[...] = jnp.where(lane == 32, square, note)
    X[z, y, head, sec, :, 0:HALF] = scaled.astype(BF16)
    msg = go(rcopy(MS, MR, m_s.at[0], m_r.at[0], at(xx=x + 1 - 2 * sec)))
    def row_ring(k, part, dim, done, fixed):
        c0, c1, c2 = PARTS[part]

        def view(a, b):
            def block(i):
                at_dim = {}
                for d in "zyx":
                    at_dim[d] = i if d == dim else None if d in done else (dims[d] + fixed.get(d, 0)) % 4
                zi, yi, xi = (slice(None) if at_dim[d] is None else at_dim[d] for d in "zyx")
                if at_dim["x"] is None:
                    return X.at[zi, yi, :, :, :, pl.ds(a, b - a)]
                return X.at[zi, yi, xi // 2, xi % 2, :, pl.ds(a, b - a)]

            return block

        return Ring(k, dim, view(c0, c2), view(c0, c1), view(c1, c2))

    first, second, third, third_own = [], [], [], []
    for part, (d1, d2, d3) in enumerate(("xyz", "yzx", "zxy")):
        k = 10 + part * 12
        first.append(row_ring(k, part, d1, "", {}))
        second.append([row_ring(k + 1 + o, part, d2, "", {d1: o}) for o in range(4)])
        third_own.append([row_ring(k + 5 + o, part, d3, "", {d1: o}) for o in range(4)])
        third.append([None] + [row_ring(k + 8 + o, part, d3, d1, {d2: o}) for o in range(1, 4)])

    def start_part(part):
        first[part].start()
        second[part][0].start()
        third_own[part][0].start()

    GU[...] = jnp.zeros_like(GU)
    start_part(0)
    start_part(1)

    msg.wait_recv()
    both = MS[...] + MR[...]
    mean_square = jnp.sum(jnp.where(lane == 32, both, 0.0), axis=1, keepdims=True) / (2 * HALF)
    inv = lax.rsqrt(mean_square + norm_epsilon)
    affinity = jax.nn.sigmoid(both * inv)
    picked = jnp.where(HIT[...] > 0.0, affinity, 0.0)
    gate = route_scale * picked / jnp.sum(picked, axis=1, keepdims=True)
    gate = jnp.where(lane == 32, inv, gate)
    top = gate.astype(BF16).astype(F32)
    X[z, y, head, sec, :, HALF:] = (top + pltpu.roll(gate - top, 64, 1)).astype(BF16)
    start_part(2)
    for part in range(3):
        first[part].forward()
        for o in (1, 3):
            second[part][o].start()
    for part in range(3):
        second[part][0].forward()
        for o in (1, 3):
            third_own[part][o].start()
    for part in range(3):
        first[part].finish()
        second[part][2].start()
        third_own[part][2].start()
    for part in range(3):
        for o in (1, 3, 2):
            second[part][o].forward()
    for part in range(3):
        third[part][1].start()
        third[part][3].start()
    far_wd(4, pl.ds(192, 64))

    to_out = []
    for d in range(1, 4):
        xx = (x + d) % 4
        s = (xx % 2) * 2 + xx // 2
        to_out.append(go(rcopy(RF.at[pl.ds(s * 4, 4)], RL.at[x], rl_s.at[d - 1], rl_r.at[d - 1], at(xx=xx))))
    RL[x] = RF[pl.ds((sec * 2 + head) * 4, 4)]
    for rings in third_own:
        for o in (0, 1, 3, 2):
            rings[o].forward()
    for before, rings in zip(second, third):
        for o in range(4):
            before[o].finish()
        rings[2].start()

    for c in send_wd:
        c.wait_recv()
    own_wd.wait()

    pass_on = []
    for i in range(4):
        pass_on.append(go(rcopy(WD.at[i, core], WD.at[i, core], wf_s.at[i], wf_r.at[i], other_core)))
    wgu_all.wait_recv()

    def cols(part):
        return PARTS[part][0], min(PARTS[part][2], HALF)

    def experts_z(zz):
        a, b = cols(0)
        for h in range(2):
            rows = X[zz, :, :, h, :, a:b].reshape(128, b - a)
            for e in range(2):
                GU[e, zz] += dot(rows, WGU[e, h, a:b]).reshape(4, 2, 16, 512)

    def experts_x(xx):
        a, b = cols(1)
        r, h = xx // 2, xx % 2
        rows = X[:, :, r, h, :, a:b].reshape(256, b - a)
        for e in range(2):
            GU[e, :, :, r] += dot(rows, WGU[e, h, a:b]).reshape(4, 4, 16, 512)

    def experts_y(yy):
        a, b = cols(2)
        for h in range(2):
            rows = X[:, yy, :, h, :, a:b].reshape(128, b - a)
            for e in range(2):
                GU[e, :, yy] += dot(rows, WGU[e, h, a:b]).reshape(4, 2, 16, 512)

    def experts(d):
        experts_z((z + d) % 4)
        experts_x((x + d) % 4)
        experts_y((y + d) % 4)

    experts(0)
    for o in (1, 3, 2):
        for rings in third:
            rings[o].forward()
    experts(1)
    experts(3)
    for o in range(4):
        for rings in third_own:
            rings[o].finish()
    for o in range(1, 4):
        for rings in third:
            rings[o].finish()
    experts(2)

    wide = lax.broadcasted_iota(jnp.int32, (128, 128), 1) % 64

    def activate(zz):
        gates = X[zz, :, :, 0, :, HALF:].reshape(128, 128).astype(F32)
        inv = jnp.sum(jnp.where(wide == 32, gates, 0.0), axis=1, keepdims=True)
        for e in range(2):
            weight = jnp.sum(jnp.where(wide == p * 2 + e, gates, 0.0), axis=1, keepdims=True)
            gu = GU[e, zz].reshape(128, 512) * inv
            act = jax.nn.silu(gu[:, :256]) * gu[:, 256:] * weight
            A[x, zz, :, :, e * 256 : e * 256 + 256] = act.astype(BF16).reshape(4, 32, 256)

    def act_ring(j):
        zz = (z + order[j]) % 4
        return Ring(
            46 + j, "x", lambda i: A.at[i, zz], lambda i: A.at[i, zz, pl.ds(0, 2)], lambda i: A.at[i, zz, pl.ds(2, 2)]
        )

    order = (2, 1, 3, 0)
    acts = [act_ring(j) for j in range(4)]
    over_y, over_z, last_z, last_y = [], [], [], []

    def down(j):
        zz = (z + order[j]) % 4
        for half, buf in ((1, Y1), (0, Y0)):
            acc = jnp.zeros((128, 896), F32)
            for i in range(4):
                acc += dot(A[i, zz].reshape(128, 512), WD[i, :, :, half * 896 : half * 896 + 896].reshape(512, 896))
            buf[j] = acc.reshape(4, 32, 896).astype(BF16)
            if half == 1 and j < 3:
                over_z.append(go(rcopy(Y1.at[j], R1.at[j], y1_s.at[j], y1_r.at[j], at(zz=zz))))
        group = []
        for m in range(3):
            yy = (y + order[m]) % 4
            group.append(go(rcopy(Y0.at[j, yy], R0.at[j, m], y0_s.at[j, m], y0_r.at[j, m], at(yy=yy))))
        over_y.append(group)

    def gather_y(j):
        zz = (z + order[j]) % 4
        for c in over_y[j]:
            c.wait_recv()
        acc = Y0[j, y].astype(F32)
        for m in range(3):
            acc += R0[j, m].astype(F32)
        if j < 3:
            T0[j] = acc.astype(BF16)
            last_z.append(go(rcopy(T0.at[j], Q0.at[j], y2_s.at[0, j], y2_r.at[0, j], at(zz=zz))))
        else:
            O0[...] = acc

    activate((z + order[0]) % 4)
    acts[0].start()
    activate((z + order[1]) % 4)
    acts[1].start()
    activate((z + order[2]) % 4)
    activate((z + order[3]) % 4)
    acts[0].forward()
    acts[2].start()
    for c in pass_on:
        c.wait_recv()
    acts[1].forward()
    acts[0].finish()
    acts[3].start()
    down(0)
    acts[2].forward()
    acts[1].finish()
    down(1)
    gather_y(0)
    acts[3].forward()
    acts[2].finish()
    down(2)
    gather_y(1)
    acts[3].finish()
    down(3)
    gather_y(2)
    for c in over_z:
        c.wait_recv()

    def sum_z(yy):
        acc = Y1[3, yy].astype(F32)
        for m in range(3):
            acc += R1[m, yy].astype(F32)
        return acc

    for m in range(3):
        yy = (y + order[m]) % 4
        T1[m] = sum_z(yy).astype(BF16)
        last_y.append(go(rcopy(T1.at[m], Q1.at[m], y2_s.at[1, m], y2_r.at[1, m], at(yy=yy))))
    gather_y(3)
    m0 = O0[...]
    m1 = sum_z(y)
    for c in to_out + last_z + last_y:
        c.wait_recv()
    for m in range(3):
        m0 += Q0[m].astype(F32)
        m1 += Q1[m].astype(F32)
    for r in range(2):
        rows = slice(r * 16, r * 16 + 16)
        low = jnp.concatenate([RL[r * 2 + h, i] for i in range(2) for h in range(2)], axis=1)
        high = jnp.concatenate([RL[r * 2 + h, i] for i in range(2, 4) for h in range(2)], axis=1)
        out_ref[rows, 0:896] = (low + m0[rows]).astype(BF16)
        out_ref[rows, 896:1792] = (high + m1[rows]).astype(BF16)

    for c in sends:
        c.wait_send()
    wgu_all.wait_send()


def body(
    hidden_in, queries, latent_cache, new_latent, cache_lengths, value_up, out_proj, norm_gain, router, expert_ids,
    w_gate_up, w_down,
):
    wgu = w_gate_up[0].reshape(7168, 2, 2, 128).transpose(0, 2, 1, 3).reshape(28672, 128)
    any_spec = pl.BlockSpec(memory_space=pl.ANY)
    vmem = pl.BlockSpec(memory_space=pltpu.VMEM)
    dma = pltpu.SemaphoreType.DMA
    return pl.pallas_call(
        layer_kernel,
        out_shape=jax.ShapeDtypeStruct((32, 1792), BF16),
        in_specs=[any_spec] * 6 + [vmem] * 5 + [pl.BlockSpec(memory_space=pltpu.SMEM)],
        out_specs=vmem,
        scratch_shapes=[
            pltpu.VMEM((2, GROUP, 208, 576), BF16),
            pltpu.VMEM((32, 32, 576), BF16),
            pltpu.VMEM((32, 576), F32),
            pltpu.VMEM((4, 1024, 128), F32),
            pltpu.VMEM((32, 512, 128), BF16),
            pltpu.VMEM((2, 3584, 128), BF16),
            pltpu.VMEM((256, 256), BF16),
            pltpu.VMEM((16, 16, 224), F32),
            pltpu.VMEM((1, HALF), F32),
            pltpu.VMEM((128, HALF), BF16),
            pltpu.VMEM((16, 128), F32),
            pltpu.VMEM((4, 4, 32, 4096), BF16),
            pltpu.VMEM((2, 224, 4096), BF16),
            pltpu.VMEM((2, 4, 4, 32, 224), F32),
            pltpu.VMEM((4, 4, 4, 16, 224), BF16),
            pltpu.VMEM((4, 4, 4, 16, 224), BF16),
            pltpu.VMEM((4, 4, 16, 224), BF16),
            pltpu.VMEM((16, 16, 224), BF16),
            pltpu.VMEM((16, 128), F32),
            pltpu.VMEM((16, 128), F32),
            pltpu.VMEM((16, 16, 224), F32),
            pltpu.VMEM((4, 4, 16, 224), F32),
            pltpu.VMEM((4, 4, 2, 2, 16, 3712), BF16),
            pltpu.VMEM((2, 2, HALF, 512), BF16),
            pltpu.VMEM((2, 4, 4, 2, 16, 512), F32),
            pltpu.VMEM((4, 2, 256, 1792), BF16),
            pltpu.VMEM((4, 4, 4, 32, 512), BF16),
            pltpu.VMEM((4, 4, 32, 896), BF16),
            pltpu.VMEM((4, 4, 32, 896), BF16),
            pltpu.VMEM((4, 3, 32, 896), BF16),
            pltpu.VMEM((3, 4, 32, 896), BF16),
            pltpu.VMEM((3, 32, 896), BF16),
            pltpu.VMEM((3, 32, 896), BF16),
            pltpu.VMEM((3, 32, 896), BF16),
            pltpu.VMEM((3, 32, 896), BF16),
            pltpu.VMEM((32, 896), F32),
            dma((50, 4)),
            dma((50, 4)),
            dma((3,)),
            dma((3,)),
            dma((15,)),
            dma((15,)),
            dma((1,)),
            dma((1,)),
            dma((3,)),
            dma((3,)),
            dma((1,)),
            dma((1,)),
            dma((1,)),
            dma((1,)),
            dma((5,)),
            dma((5,)),
            dma((4,)),
            dma((4,)),
            dma((4, 3)),
            dma((4, 3)),
            dma((3,)),
            dma((3,)),
            dma((2, 3)),
            dma((2, 3)),
            dma((4,)),
            dma((2,)),
            dma((2,)),
        ],
        compiler_params=pltpu.CompilerParams(
            collective_id=0, has_side_effects=True, vmem_limit_bytes=66_000_000
        ),
        name="layer",
    )(
        queries, latent_cache, value_up, out_proj.T, wgu, w_down[0], new_latent, hidden_in, norm_gain.reshape(1, -1),
        router.T, expert_ids.T, cache_lengths,
    )


def solution(mesh):
    in_specs = (
        P("batch", None),
        P("batch", ("sec", "head"), None),
        P("batch", None, None),
        P("batch", None),
        P("batch"),
        P(("sec", "head"), None, None),
        P(("sec", "head"), "batch"),
        P(),
        P(),
        P("batch", None),
        P("batch", None, None, ("sec", "head")),
        P("batch", ("sec", "head"), None),
    )
    out_specs = P("batch", ("sec", "head"))
    return jax.shard_map(body, mesh=mesh, in_specs=in_specs, out_specs=out_specs, check_vma=False)
```
